32 devices in a mesh: dp: 8 (over y, x, core), tensor: 4 (over z).
Axes of the slice: x: 2, y: 2, z: 4, core: 2. Of those that a mesh axis runs over, the one named last changes fastest.
Arguments:
- block_input: float32 [12544, 512], P(('dp', 'tensor')), as said below
- cotangent: float32 [12544, 512], P(('dp', 'tensor')), may hold values from -6 to 6
- w_qkv: bfloat16 [2, 512, 3, 512], P(None, 'dp', None, 'tensor'), may hold values from -0.25 to 0.25
- b_qv: bfloat16 [2, 2, 512], P(None, None, 'tensor'), may hold values from -3 to 3
- bias_table: bfloat16 [2, 169, 16], P(None, None, 'tensor'), may hold values from -4 to 4
- w_proj: bfloat16 [2, 512, 512], P(None, 'tensor', 'dp'), may hold values from -0.75 to 0.75
- w_fc1: bfloat16 [2, 512, 2048], P(None, 'dp', 'tensor'), may hold values from -0.25 to 0.25
- b_fc1: bfloat16 [2, 2048], P(None, 'tensor'), may hold values from -3 to 3
- w_fc2: bfloat16 [2, 2048, 512], P(None, 'tensor', 'dp'), may hold values from -0.1875 to 0.1875
- norm_params: bfloat16 [2, 6, 512], P(None, None, 'dp'), as said below
- rel_index: int32 [49, 49], replicated, may hold values from 0 to 168, as said below
- shift_perm: int32 [196], replicated, may hold values from 0 to 195, as said below
- shift_mask: int32 [4, 49, 49], replicated, may hold values from 0 to 1, as said below
Outputs:
- block_output: float32 [12544, 512], P(('dp', 'tensor'))
- d_block_input: float32 [12544, 512], P(('dp', 'tensor'))
- d_w_qkv: float32 [2, 512, 3, 512], P(None, 'dp', None, 'tensor')
- d_b_qv: float32 [2, 2, 512], P(None, None, 'tensor')
- d_bias_table: float32 [2, 169, 16], P(None, None, 'tensor')
- d_w_proj: float32 [2, 512, 512], P(None, 'tensor', 'dp')
- d_w_fc1: float32 [2, 512, 2048], P(None, 'dp', 'tensor')
- d_b_fc1: float32 [2, 2048], P(None, 'tensor')
- d_w_fc2: float32 [2, 2048, 512], P(None, 'tensor', 'dp')
- d_norm_params: float32 [2, 6, 512], P(None, None, 'dp')
The draws below stay inside these ranges and needn't reach their ends.
Inputs may be any that keep to these rules, and one draw needn't show every extreme that they name: `block_input`: standard normal scaled by a factor per token and a factor per feature. `norm_params`: rows 0 and 3 are positive gains. `rel_index`: two pairs of window positions have equal entries exactly when they have the same row offset and the same column offset; every value appears. A permutation: the image is rolled cyclically by amounts of 1 to 6 tokens, drawn once, along both grid dimensions, and cut into windows; window-ordered position j of the rolled image holds the token whose window-ordered position is shift_perm[j]. `shift_mask`: 1 where two positions of a window of the rolled image of shift_perm lie in different regions of the shifted-window partition for that roll, else 0; zero on the diagonal.
All inputs are finite; a program needn't handle non-finite values.
Results may differ from the reference program's by a relative error of at most 0.022.
Values may be sent and summed in bfloat16 or wider, within the bound.
No kernel may reach another device: no remote copies, remote signals or barrier semaphores. Data moves between devices by JAX's collectives and lax.ppermute only.
A program may use at most 192 MiB of HBM per device.

```python
import jax
import jax.numpy as jnp
from jax import lax

D = 512
HEADS = 16
FF = 2048
WIN = 7
SIDE = 14
IMG_DEV = 8
HEAD_DIM = 32
WTOK = 49
ITOK = 196
NWIN = 4
RELS = 169
TOKENS = 12544
N_DP = 8


def shift_amounts(key):
    sub_key = jax.random.fold_in(key, 11)
    return jax.random.randint(sub_key, (2,), 1, WIN, dtype=jnp.int32)


def window_grid():
    position = jnp.arange(ITOK, dtype=jnp.int32)
    window = position // WTOK
    inside = position % WTOK
    per_row = SIDE // WIN
    row_index = window // per_row * WIN + inside // WIN
    col_index = window % per_row * WIN + inside % WIN
    return (row_index, col_index)


def draw_shift_perm(key, part):
    amounts = shift_amounts(key)
    row_index, col_index = window_grid()
    source_row = (row_index + amounts[0]) % SIDE
    source_col = (col_index + amounts[1]) % SIDE
    per_row = SIDE // WIN
    return ((source_row // WIN * per_row + source_col // WIN) * WTOK + source_row % WIN * WIN + source_col % WIN).astype(jnp.int32)


def draw_shift_mask(key, part):
    amounts = shift_amounts(key)
    row_index, col_index = window_grid()
    row_region = jnp.where(row_index < SIDE - WIN, 0, jnp.where(row_index < SIDE - amounts[0], 1, 2))
    col_region = jnp.where(col_index < SIDE - WIN, 0, jnp.where(col_index < SIDE - amounts[1], 1, 2))
    region_label = (row_region * 3 + col_region).reshape(NWIN, WTOK)
    return (region_label[:, :, None] != region_label[:, None, :]).astype(jnp.int32)


def draw_rel_index(key, part):
    relabel = jax.random.permutation(jax.random.fold_in(key, 5), RELS).astype(jnp.int32)
    inside = jnp.arange(WTOK, dtype=jnp.int32)
    row_index = inside // WIN
    col_index = inside % WIN
    row_offset = row_index[:, None] - row_index[None, :] + WIN - 1
    col_offset = col_index[:, None] - col_index[None, :] + WIN - 1
    return relabel[row_offset * (2 * WIN - 1) + col_offset]


def draw_block_input(key, part):
    first_key, second_key, third_key = jax.random.split(jax.random.fold_in(key, 3), 3)
    values = jax.random.normal(first_key, (TOKENS, D), jnp.float32)
    row_scale = jnp.exp(jax.random.uniform(second_key, (TOKENS, 1), jnp.float32, -1.15, 1.15))
    col_scale = jnp.exp(jax.random.uniform(third_key, (1, D), jnp.float32, -0.5, 0.5))
    return values * row_scale * col_scale


def draw_norm_params(key, part):
    first_key, second_key = jax.random.split(jax.random.fold_in(key, 17), 2)
    gain_values = jax.random.uniform(first_key, (2, 6, D), jnp.float32, 0.6, 1.4)
    shifts = 0.5 * jax.random.normal(second_key, (2, 6, D), jnp.float32)
    row_index = jnp.arange(6)
    is_gain = ((row_index == 0) | (row_index == 3))[None, :, None]
    return jnp.where(is_gain, gain_values, shifts).astype(jnp.bfloat16)


def strengthened(drawn, rng, source, target, shards_of, factor):
    def block_of(dim):
        return (jnp.arange(drawn.shape[dim]) // (drawn.shape[dim] // shards_of)).reshape((-1,) + (1,) * (drawn.ndim - 1 - dim))

    near = jax.random.permutation(rng, shards_of)[block_of(target)]
    far = (block_of(target) + shards_of // 2) % shards_of
    return jnp.where((block_of(source) == near) | (block_of(source) == far), factor * drawn, drawn)


def block_scale(stream_key, extent, cuts, smallest, largest):
    def one(axis_at, shards_of):
        draws = jax.random.uniform(jax.random.fold_in(jax.random.fold_in(stream_key, 6), axis_at), (shards_of,), jnp.float32, smallest / len(cuts), largest / len(cuts))
        return jnp.repeat(jnp.exp(draws), extent[axis_at] // shards_of).reshape((-1,) + (1,) * (len(extent) - axis_at - 1))

    gain = one(*cuts[0])
    for cut in cuts[1:]:
        gain = gain * one(*cut)
    return gain


def normal_values(own_key, dims, width, reach, cuts=(), kind=jnp.bfloat16):
    gain = block_scale(own_key, dims, cuts, -0.22, 0.18) if cuts else 1.0
    entries = jax.random.normal(own_key, dims, jnp.float32) * width * gain
    return jnp.minimum(jnp.maximum(entries, -reach), reach).astype(kind)


def gaussian_with(rng, shape, scale, most, shards, heavy, kind=jnp.bfloat16):
    values = scale * jax.random.normal(rng, shape, jnp.float32)
    if shards:
        values = values * block_scale(rng, shape, shards, -0.22, 0.18)
    return jnp.clip(strengthened(values, jax.random.fold_in(rng, 3), *heavy), -most, most).astype(kind)


def setup_inputs(seed: int = 0) -> dict:
    keys = jax.random.split(jax.random.key(seed), 14)
    return {
        "block_input": draw_block_input(jax.random.fold_in(keys[13], 71), 0),
        "cotangent": gaussian_with(keys[1], (TOKENS, D), 1.0, 6.0, ((0, 32),), (0, 1, 32, 2.75), jnp.float32),
        "w_qkv": normal_values(keys[2], (2, D, 3, D), D ** -0.5, 0.25, ((1, 8), (3, 4))),
        "b_qv": normal_values(keys[3], (2, 2, D), 0.5, 3.0, ((2, 4),)),
        "bias_table": normal_values(keys[4], (2, RELS, HEADS), 1.0, 4.0, ((2, 4),)),
        "w_proj": normal_values(keys[5], (2, D, D), (D // 8) ** -0.5, 0.75, ((1, 4), (2, 8))),
        "w_fc1": normal_values(keys[6], (2, D, FF), D ** -0.5, 0.25, ((1, 8), (2, 4))),
        "b_fc1": normal_values(keys[7], (2, FF), 0.5, 3.0, ((1, 4),)),
        "w_fc2": normal_values(keys[8], (2, FF, D), (FF // 2) ** -0.5, 0.1875, ((1, 4), (2, 8))),
        "norm_params": draw_norm_params(jax.random.fold_in(keys[13], 71), 0),
        "rel_index": draw_rel_index(jax.random.fold_in(keys[13], 71), 0),
        "shift_perm": draw_shift_perm(jax.random.fold_in(keys[13], 71), 0),
        "shift_mask": draw_shift_mask(jax.random.fold_in(keys[13], 71), 0),
    }


EPS = 1e-05
MASKED = -100.0
ROOT_HALF = 0.7071067811865476
ROOT_TWO_PI = 2.5066282746310002
full_precision = lax.Precision.HIGHEST

def gelu_value(inputs):
    return inputs * 0.5 * (1.0 + lax.erf(inputs * ROOT_HALF))

def gelu_slope(inputs):
    return 0.5 * (1.0 + lax.erf(inputs * ROOT_HALF)) + inputs * jnp.exp(-0.5 * inputs * inputs) / ROOT_TWO_PI

def layer_norm(hidden, norm_gain, offset):
    row_mean = lax.optimization_barrier(jnp.mean(hidden, axis=-1, keepdims=True))
    centred = hidden - row_mean
    inv_std = lax.rsqrt(lax.optimization_barrier(jnp.mean(centred * centred, axis=-1, keepdims=True)) + EPS)
    normed = centred * inv_std
    return (normed * norm_gain + offset, normed, inv_std)

def norm_back(grad_rows, normed, inv_std, norm_gain):
    scaled = grad_rows * norm_gain
    centred_grad = scaled - lax.optimization_barrier(jnp.mean(scaled, axis=-1, keepdims=True)) - normed * lax.optimization_barrier(jnp.mean(scaled * normed, axis=-1, keepdims=True))
    return inv_std * centred_grad

def inner_rows(left_side, right_side):
    return lax.dot_general(left_side, right_side, (((0,), (0,)), ((), ())), preferred_element_type=jnp.float32)

def times_transposed(left_side, right_side):
    return lax.dot_general(left_side, right_side, (((1,), (1,)), ((), ())), preferred_element_type=jnp.float32)

def rel_lookup(rel_index):
    flat_cells = rel_index.reshape(-1).astype(jnp.int32)
    return (flat_cells[:, None] == jnp.arange(RELS, dtype=jnp.int32)[None, :]).astype(jnp.float32)

def position_bias(lookup, pos_table):
    head_count = pos_table.shape[-1]
    flat_bias = jnp.dot(lookup, pos_table.astype(jnp.float32), precision=full_precision)
    return flat_bias.reshape(WTOK, WTOK, head_count).transpose(2, 0, 1)

def window_scores(query_blocks, key_blocks, pos_bias, mask_term):
    scores = jnp.einsum('inqhe,inkhe->inhqk', query_blocks.astype(jnp.float32), key_blocks.astype(jnp.float32))
    scores = scores + pos_bias[None, None]
    if mask_term is not None:
        scores = scores + mask_term[None, :, None]
    return scores

def forward_layer(hidden, weights, lookup, mask_term, reorder):
    w_qkv, b_qv, pos_table, w_proj, w_fc1, b_fc1, w_fc2, norm_rows = weights
    norm_rows = norm_rows.astype(jnp.float32)
    local_width = w_qkv.shape[-1]
    head_count = local_width // HEAD_DIM
    score_scale = HEAD_DIM ** (-0.5)
    ln_first, normed_first, inv_first = layer_norm(hidden, norm_rows[0], norm_rows[1])
    gathered = ln_first.astype(jnp.bfloat16)
    image_count = gathered.shape[0] // ITOK
    arranged = gathered.reshape(image_count, ITOK, D)
    if reorder is not None:
        arranged = jnp.take(arranged, reorder[0], axis=1)
    permuted_rows = arranged.reshape(image_count * ITOK, D)
    projected = jnp.dot(permuted_rows, w_qkv.reshape(D, 3 * local_width), preferred_element_type=jnp.float32)
    projected = projected.reshape(-1, 3, local_width)
    biases = b_qv.astype(jnp.float32)
    query_rows = ((projected[:, 0] + biases[0]) * score_scale).astype(jnp.bfloat16)
    key_rows = projected[:, 1].astype(jnp.bfloat16)
    value_rows = (projected[:, 2] + biases[1]).astype(jnp.bfloat16)
    block_shape = (image_count, NWIN, WTOK, head_count, HEAD_DIM)
    query_blocks = query_rows.reshape(block_shape)
    key_blocks = key_rows.reshape(block_shape)
    value_blocks = value_rows.reshape(block_shape)
    pos_bias = position_bias(lookup, pos_table)
    scores = window_scores(query_blocks, key_blocks, pos_bias, mask_term)
    row_peak = lax.optimization_barrier(jnp.max(scores, axis=-1, keepdims=True))
    log_total = row_peak + jnp.log(lax.optimization_barrier(jnp.sum(jnp.exp(scores - row_peak), axis=-1, keepdims=True)))
    soft_weights = jnp.exp(scores - log_total).astype(jnp.bfloat16)
    mixed = jnp.einsum('inhqk,inkhe->inqhe', soft_weights.astype(jnp.float32), value_blocks.astype(jnp.float32)).astype(jnp.bfloat16)
    mixed = mixed.reshape(image_count, ITOK, local_width)
    if reorder is not None:
        mixed = jnp.take(mixed, reorder[1], axis=1)
    mixed = mixed.reshape(image_count * ITOK, local_width)
    residual = hidden + jnp.dot(mixed, w_proj, preferred_element_type=jnp.float32) + norm_rows[2]
    ln_second, normed_second, inv_second = layer_norm(residual, norm_rows[3], norm_rows[4])
    spread = ln_second.astype(jnp.bfloat16)
    pre_active = jnp.dot(spread, w_fc1, preferred_element_type=jnp.float32) + b_fc1.astype(jnp.float32)
    active = gelu_value(pre_active).astype(jnp.bfloat16)
    result = residual + jnp.dot(active, w_fc2, preferred_element_type=jnp.float32) + norm_rows[5]
    kept_state = (normed_first, inv_first, permuted_rows, query_blocks, key_blocks, value_blocks, log_total, mixed, normed_second, inv_second, spread, pre_active, active)
    return (result, kept_state)

def backward_layer(out_grad, kept_state, weights, lookup, mask_term, reorder):
    normed_first, inv_first, permuted_rows, query_blocks, key_blocks, value_blocks, log_total, mixed, normed_second, inv_second, spread, pre_active, active = kept_state
    w_qkv, b_qv, pos_table, w_proj, w_fc1, b_fc1, w_fc2, norm_rows = weights
    norm_rows = norm_rows.astype(jnp.float32)
    local_width = w_qkv.shape[-1]
    head_count = local_width // HEAD_DIM
    score_scale = HEAD_DIM ** (-0.5)
    image_count = permuted_rows.shape[0] // ITOK
    grad_rounded = out_grad.astype(jnp.bfloat16)
    d_fc2 = inner_rows(active, grad_rounded)
    d_active = times_transposed(grad_rounded, w_fc2)
    d_pre = d_active * gelu_slope(pre_active)
    d_bias_fc1 = lax.optimization_barrier(jnp.sum(d_pre, axis=0))
    d_pre_rounded = d_pre.astype(jnp.bfloat16)
    d_fc1 = inner_rows(spread, d_pre_rounded)
    d_spread = times_transposed(d_pre_rounded, w_fc1)
    d_residual = out_grad + norm_back(d_spread, normed_second, inv_second, norm_rows[3])
    mix_grad = d_residual.astype(jnp.bfloat16)
    d_proj = inner_rows(mixed, mix_grad)
    d_mixed = times_transposed(mix_grad, w_proj).astype(jnp.bfloat16).reshape(image_count, ITOK, local_width)
    if reorder is not None:
        d_mixed = jnp.take(d_mixed, reorder[0], axis=1)
    d_mixed_blocks = d_mixed.reshape(image_count, NWIN, WTOK, head_count, HEAD_DIM).astype(jnp.float32)
    pos_bias = position_bias(lookup, pos_table)
    scores = window_scores(query_blocks, key_blocks, pos_bias, mask_term)
    soft_exact = jnp.exp(scores - log_total)
    soft_rounded = soft_exact.astype(jnp.bfloat16).astype(jnp.float32)
    d_values = jnp.einsum('inhqk,inqhe->inkhe', soft_rounded, d_mixed_blocks)
    d_soft = jnp.einsum('inqhe,inkhe->inhqk', d_mixed_blocks, value_blocks.astype(jnp.float32))
    d_scores = soft_exact * (d_soft - lax.optimization_barrier(jnp.sum(soft_exact * d_soft, axis=-1, keepdims=True)))
    score_total = lax.optimization_barrier(jnp.sum(d_scores, axis=(0, 1))).reshape(head_count, WTOK * WTOK)
    d_table = jnp.dot(lookup.T, score_total.T, precision=full_precision)
    d_scores_rounded = d_scores.astype(jnp.bfloat16).astype(jnp.float32)
    d_query = jnp.einsum('inhqk,inkhe->inqhe', d_scores_rounded, key_blocks.astype(jnp.float32)) * score_scale
    d_keys = jnp.einsum('inhqk,inqhe->inkhe', d_scores_rounded, query_blocks.astype(jnp.float32))
    d_query = d_query.reshape(-1, local_width)
    d_keys = d_keys.reshape(-1, local_width)
    d_values = d_values.reshape(-1, local_width)
    d_bias_qv = jnp.stack([lax.optimization_barrier(jnp.sum(d_query, axis=0)), lax.optimization_barrier(jnp.sum(d_values, axis=0))])
    d_joint = jnp.stack([d_query, d_keys, d_values], axis=1).astype(jnp.bfloat16).reshape(-1, 3 * local_width)
    d_qkv = inner_rows(permuted_rows, d_joint).reshape(D, 3, local_width)
    d_normed = times_transposed(d_joint, w_qkv.reshape(D, 3 * local_width))
    if reorder is not None:
        d_normed = jnp.take(d_normed.reshape(image_count, ITOK, D), reorder[1], axis=1).reshape(image_count * ITOK, D)
    d_hidden = d_residual + norm_back(d_normed, normed_first, inv_first, norm_rows[0])
    norm_grads = jnp.stack([lax.optimization_barrier(jnp.sum(d_normed * normed_first, axis=0)), lax.optimization_barrier(jnp.sum(d_normed, axis=0)), lax.optimization_barrier(jnp.sum(d_residual, axis=0)), lax.optimization_barrier(jnp.sum(d_spread * normed_second, axis=0)), lax.optimization_barrier(jnp.sum(d_spread, axis=0)), lax.optimization_barrier(jnp.sum(out_grad, axis=0))])
    return (d_hidden, (d_qkv, d_bias_qv, d_table, d_proj, d_fc1, d_bias_fc1, d_fc2, norm_grads))

def reference(block_input, cotangent, w_qkv, b_qv, bias_table, w_proj, w_fc1, b_fc1, w_fc2, norm_params, rel_index, shift_perm, shift_mask):
    perm_index = shift_perm.astype(jnp.int32)
    inverse = jnp.zeros((ITOK,), jnp.int32).at[perm_index].set(jnp.arange(ITOK, dtype=jnp.int32))
    reorder = (perm_index, inverse)
    lookup = rel_lookup(rel_index)
    mask_term = shift_mask.astype(jnp.float32) * MASKED

    def weights_of(layer_index):
        return (w_qkv[layer_index], b_qv[layer_index], bias_table[layer_index], w_proj[layer_index], w_fc1[layer_index], b_fc1[layer_index], w_fc2[layer_index], norm_params[layer_index])

    def block_step(totals, pieces):
        hidden, out_grad = pieces
        first_out, kept_first = forward_layer(hidden, weights_of(0), lookup, None, None)
        second_out, kept_second = forward_layer(first_out, weights_of(1), lookup, mask_term, reorder)
        grad_mid, grads_second = backward_layer(out_grad, kept_second, weights_of(1), lookup, mask_term, reorder)
        grad_in, grads_first = backward_layer(grad_mid, kept_first, weights_of(0), lookup, None, None)
        totals = jax.tree.map(lambda total, earlier, later: total + jnp.stack([earlier, later]), totals, grads_first, grads_second)
        return (totals, (second_out, grad_in))
    initial = (jnp.zeros((2, D, 3, D), jnp.float32), jnp.zeros((2, 2, D), jnp.float32), jnp.zeros((2, RELS, HEADS), jnp.float32), jnp.zeros((2, D, D), jnp.float32), jnp.zeros((2, D, FF), jnp.float32), jnp.zeros((2, FF), jnp.float32), jnp.zeros((2, FF, D), jnp.float32), jnp.zeros((2, 6, D), jnp.float32))
    pieces = (block_input.reshape(N_DP, IMG_DEV * ITOK, D), cotangent.reshape(N_DP, IMG_DEV * ITOK, D))
    totals, (outputs, grads_in) = lax.scan(block_step, initial, pieces)
    d_qkv, d_bias_qv, d_table, d_proj, d_fc1, d_bias_fc1, d_fc2, d_norms = totals
    return (outputs.reshape(TOKENS, D), grads_in.reshape(TOKENS, D), d_qkv, d_bias_qv, d_table, d_proj, d_fc1, d_bias_fc1, d_fc2, d_norms)
```

```python
import jax
import jax.numpy as jnp
from jax import lax
from jax.sharding import PartitionSpec as P

D = 512
HEAD_DIM = 32
WTOK = 49
ITOK = 196
NWIN = 4
RELS = 169


EPS = 1e-05
MASKED = -100.0
ROOT_HALF = 0.7071067811865476
ROOT_TWO_PI = 2.5066282746310002
full_precision = lax.Precision.HIGHEST


def gelu_value(inputs):
    return inputs * 0.5 * (1.0 + lax.erf(inputs * ROOT_HALF))


def gelu_slope(inputs):
    return (
        0.5 * (1.0 + lax.erf(inputs * ROOT_HALF))
        + inputs * jnp.exp(-0.5 * inputs * inputs) / ROOT_TWO_PI
    )


def layer_norm(hidden, norm_gain, offset):
    row_mean = jnp.mean(hidden, axis=-1, keepdims=True)
    centred = hidden - row_mean
    inv_std = lax.rsqrt(jnp.mean(centred * centred, axis=-1, keepdims=True) + EPS)
    normed = centred * inv_std
    return (normed * norm_gain + offset, normed, inv_std)


def norm_back(grad_rows, normed, inv_std, norm_gain):
    scaled = grad_rows * norm_gain
    centred_grad = (
        scaled
        - jnp.mean(scaled, axis=-1, keepdims=True)
        - normed * jnp.mean(scaled * normed, axis=-1, keepdims=True)
    )
    return inv_std * centred_grad


def inner_rows(left_side, right_side):
    return lax.dot_general(
        left_side, right_side, (((0,), (0,)), ((), ())), preferred_element_type=jnp.float32
    )


def times_transposed(left_side, right_side):
    return lax.dot_general(
        left_side, right_side, (((1,), (1,)), ((), ())), preferred_element_type=jnp.float32
    )


def rel_lookup(rel_index):
    flat_cells = rel_index.reshape(-1)
    return (flat_cells[:, None] == jnp.arange(RELS, dtype=jnp.int32)[None, :]).astype(jnp.float32)


def position_bias(lookup, pos_table):
    head_count = pos_table.shape[-1]
    flat_bias = jnp.dot(lookup, pos_table.astype(jnp.float32), precision=full_precision)
    return flat_bias.reshape(WTOK, WTOK, head_count).transpose(2, 0, 1)


def window_scores(query_blocks, key_blocks, pos_bias, mask_term):
    scores = jnp.einsum(
        "inqhe,inkhe->inhqk", query_blocks, key_blocks, preferred_element_type=jnp.float32
    )
    scores = scores + pos_bias[None, None]
    if mask_term is not None:
        scores = scores + mask_term[None, :, None]
    return scores


def spread_rows(values):
    return values


def spread_grads(values):
    return values


def branch_sum(values, weight):
    return jnp.dot(values, weight, preferred_element_type=jnp.float32)


def back_sum(values, weight):
    return times_transposed(values, weight)


def gather_both(shard, dp_dim, tensor_dim):
    gathered = lax.all_gather(shard, ("dp", "tensor"), axis=0, tiled=False)
    return join_blocks(gathered, dp_dim, tensor_dim)


def join_blocks(gathered, dp_dim, tensor_dim):
    n_dp, n_tensor = lax.axis_size("dp"), lax.axis_size("tensor")
    shape = gathered.shape[1:]
    blocks = gathered.reshape((n_dp, n_tensor) + shape)
    order = []
    final = []
    for dim, size in enumerate(shape):
        if dim == dp_dim:
            order.append(0)
            size *= n_dp
        if dim == tensor_dim:
            order.append(1)
            size *= n_tensor
        order.append(dim + 2)
        final.append(size)
    return blocks.transpose(order).reshape(final)


def scatter_both(grads, dp_dim, tensor_dim):
    n_dp, n_tensor = lax.axis_size("dp"), lax.axis_size("tensor")
    split = []
    front = [None, None]
    rest = []
    for dim, size in enumerate(grads.shape):
        if dim == dp_dim:
            front[0] = len(split)
            split.append(n_dp)
            size //= n_dp
        if dim == tensor_dim:
            front[1] = len(split)
            split.append(n_tensor)
            size //= n_tensor
        rest.append(len(split))
        split.append(size)
    blocks = grads.astype(jnp.bfloat16).reshape(split).transpose(front + rest)
    shape = blocks.shape[2:]
    part = lax.psum_scatter(blocks, "dp", scatter_dimension=0, tiled=False)
    part = lax.psum_scatter(part, "tensor", scatter_dimension=0, tiled=False)
    return part.reshape(shape).astype(jnp.float32)


def forward_layer(hidden, weights, lookup, mask_term, reorder):
    w_qkv, b_qv, pos_table, w_proj, w_fc1, b_fc1, w_fc2, norm_rows = weights
    norm_rows = norm_rows.astype(jnp.float32)
    local_width = w_qkv.shape[-1]
    head_count = local_width // HEAD_DIM
    score_scale = HEAD_DIM ** (-0.5)
    ln_first, normed_first, inv_first = layer_norm(hidden, norm_rows[0], norm_rows[1])
    gathered = spread_rows(ln_first.astype(jnp.bfloat16))
    image_count = gathered.shape[0] // ITOK
    arranged = gathered.reshape(image_count, ITOK, D)
    if reorder is not None:
        arranged = jnp.take(arranged, reorder[0], axis=1)
    permuted_rows = arranged.reshape(image_count * ITOK, D)
    projected = jnp.dot(
        permuted_rows, w_qkv.reshape(D, 3 * local_width), preferred_element_type=jnp.float32
    )
    projected = projected.reshape(-1, 3, local_width)
    biases = b_qv.astype(jnp.float32)
    query_rows = ((projected[:, 0] + biases[0]) * score_scale).astype(jnp.bfloat16)
    key_rows = projected[:, 1].astype(jnp.bfloat16)
    value_rows = (projected[:, 2] + biases[1]).astype(jnp.bfloat16)
    block_shape = (image_count, NWIN, WTOK, head_count, HEAD_DIM)
    query_blocks = query_rows.reshape(block_shape)
    key_blocks = key_rows.reshape(block_shape)
    value_blocks = value_rows.reshape(block_shape)
    pos_bias = position_bias(lookup, pos_table)
    scores = window_scores(query_blocks, key_blocks, pos_bias, mask_term)
    row_peak = jnp.max(scores, axis=-1, keepdims=True)
    log_total = row_peak + jnp.log(jnp.sum(jnp.exp(scores - row_peak), axis=-1, keepdims=True))
    soft_weights = jnp.exp(scores - log_total).astype(jnp.bfloat16)
    mixed = jnp.einsum(
        "inhqk,inkhe->inqhe", soft_weights, value_blocks, preferred_element_type=jnp.float32
    ).astype(jnp.bfloat16)
    mixed = mixed.reshape(image_count, ITOK, local_width)
    if reorder is not None:
        mixed = jnp.take(mixed, reorder[1], axis=1)
    mixed = mixed.reshape(image_count * ITOK, local_width)
    residual = hidden + branch_sum(mixed, w_proj) + norm_rows[2]
    ln_second, normed_second, inv_second = layer_norm(residual, norm_rows[3], norm_rows[4])
    spread = spread_rows(ln_second.astype(jnp.bfloat16))
    pre_active = jnp.dot(spread, w_fc1, preferred_element_type=jnp.float32) + b_fc1.astype(
        jnp.float32
    )
    active = gelu_value(pre_active).astype(jnp.bfloat16)
    result = residual + branch_sum(active, w_fc2) + norm_rows[5]
    kept_state = (
        normed_first,
        inv_first,
        permuted_rows,
        query_blocks,
        key_blocks,
        value_blocks,
        log_total,
        mixed,
        normed_second,
        inv_second,
        spread,
        pre_active,
        active,
    )
    return (result, kept_state)


def backward_layer(out_grad, kept_state, weights, lookup, mask_term, reorder):
    (
        normed_first,
        inv_first,
        permuted_rows,
        query_blocks,
        key_blocks,
        value_blocks,
        log_total,
        mixed,
        normed_second,
        inv_second,
        spread,
        pre_active,
        active,
    ) = kept_state
    w_qkv, b_qv, pos_table, w_proj, w_fc1, b_fc1, w_fc2, norm_rows = weights
    norm_rows = norm_rows.astype(jnp.float32)
    local_width = w_qkv.shape[-1]
    head_count = local_width // HEAD_DIM
    score_scale = HEAD_DIM ** (-0.5)
    image_count = permuted_rows.shape[0] // ITOK
    grad_rounded = spread_grads(out_grad.astype(jnp.bfloat16))
    d_fc2 = inner_rows(active, grad_rounded)
    d_active = times_transposed(grad_rounded, w_fc2)
    d_pre = d_active * gelu_slope(pre_active)
    d_bias_fc1 = jnp.sum(d_pre, axis=0)
    d_pre_rounded = d_pre.astype(jnp.bfloat16)
    d_fc1 = inner_rows(spread, d_pre_rounded)
    d_spread = back_sum(d_pre_rounded, w_fc1)
    d_residual = out_grad + norm_back(d_spread, normed_second, inv_second, norm_rows[3])
    mix_grad = spread_grads(d_residual.astype(jnp.bfloat16))
    d_proj = inner_rows(mixed, mix_grad)
    d_mixed = (
        times_transposed(mix_grad, w_proj)
        .astype(jnp.bfloat16)
        .reshape(image_count, ITOK, local_width)
    )
    if reorder is not None:
        d_mixed = jnp.take(d_mixed, reorder[0], axis=1)
    d_mixed_blocks = d_mixed.reshape(image_count, NWIN, WTOK, head_count, HEAD_DIM)
    pos_bias = position_bias(lookup, pos_table)
    scores = window_scores(query_blocks, key_blocks, pos_bias, mask_term)
    soft_exact = jnp.exp(scores - log_total)
    d_values = jnp.einsum(
        "inhqk,inqhe->inkhe",
        soft_exact.astype(jnp.bfloat16),
        d_mixed_blocks,
        preferred_element_type=jnp.float32,
    )
    d_soft = jnp.einsum(
        "inqhe,inkhe->inhqk", d_mixed_blocks, value_blocks, preferred_element_type=jnp.float32
    )
    d_scores = soft_exact * (d_soft - jnp.sum(soft_exact * d_soft, axis=-1, keepdims=True))
    score_total = jnp.sum(d_scores, axis=(0, 1)).reshape(head_count, WTOK * WTOK)
    d_table = jnp.dot(lookup.T, score_total.T, precision=full_precision)
    d_scores_rounded = d_scores.astype(jnp.bfloat16)
    d_query = (
        jnp.einsum(
            "inhqk,inkhe->inqhe", d_scores_rounded, key_blocks, preferred_element_type=jnp.float32
        )
        * score_scale
    )
    d_keys = jnp.einsum(
        "inhqk,inqhe->inkhe", d_scores_rounded, query_blocks, preferred_element_type=jnp.float32
    )
    d_query = d_query.reshape(-1, local_width)
    d_keys = d_keys.reshape(-1, local_width)
    d_values = d_values.reshape(-1, local_width)
    d_bias_qv = jnp.stack([jnp.sum(d_query, axis=0), jnp.sum(d_values, axis=0)])
    d_joint = (
        jnp.stack([d_query, d_keys, d_values], axis=1)
        .astype(jnp.bfloat16)
        .reshape(-1, 3 * local_width)
    )
    d_qkv = inner_rows(permuted_rows, d_joint).reshape(D, 3, local_width)
    if reorder is not None:
        d_joint = jnp.take(
            d_joint.reshape(image_count, ITOK, 3 * local_width), reorder[1], axis=1
        ).reshape(image_count * ITOK, 3 * local_width)
    d_normed = back_sum(d_joint, w_qkv.reshape(D, 3 * local_width))
    d_hidden = d_residual + norm_back(d_normed, normed_first, inv_first, norm_rows[0])
    norm_grads = jnp.stack(
        [
            jnp.sum(d_normed * normed_first, axis=0),
            jnp.sum(d_normed, axis=0),
            jnp.sum(d_residual, axis=0),
            jnp.sum(d_spread * normed_second, axis=0),
            jnp.sum(d_spread, axis=0),
            jnp.sum(out_grad, axis=0),
        ]
    )
    return (d_hidden, (d_qkv, d_proj, d_fc1, d_fc2), (d_bias_qv, d_table, d_bias_fc1), norm_grads)


def join_two(first_item, second_item):
    return jnp.concatenate([first_item, second_item], axis=0)


def body(
    block_input,
    cotangent,
    w_qkv,
    b_qv,
    bias_table,
    w_proj,
    w_fc1,
    b_fc1,
    w_fc2,
    norm_params,
    rel_index,
    shift_perm,
    shift_mask,
):
    full_qkv, full_proj, full_fc1, full_fc2 = (
        gather_both(w_qkv, 1, 3),
        gather_both(w_proj, 2, 1),
        gather_both(w_fc1, 1, 2),
        gather_both(w_fc2, 2, 1),
    )
    norm_rows = lax.all_gather(norm_params, "dp", axis=2, tiled=True)
    head_bias = lax.all_gather(b_qv, "tensor", axis=2, tiled=True)
    pos_table = lax.all_gather(bias_table, "tensor", axis=2, tiled=True)
    fc1_bias = lax.all_gather(b_fc1, "tensor", axis=1, tiled=True)
    inverse = jnp.zeros((ITOK,), jnp.int32).at[shift_perm].set(jnp.arange(ITOK, dtype=jnp.int32))
    reorder = (shift_perm, inverse)
    lookup = rel_lookup(rel_index)
    mask_term = shift_mask.astype(jnp.float32) * MASKED

    def weights_of(layer_index):
        return (
            full_qkv[layer_index],
            head_bias[layer_index],
            pos_table[layer_index],
            full_proj[layer_index],
            full_fc1[layer_index],
            fc1_bias[layer_index],
            full_fc2[layer_index],
            norm_rows[layer_index],
        )

    first_out, kept_first = forward_layer(block_input, weights_of(0), lookup, None, None)
    second_out, kept_second = forward_layer(first_out, weights_of(1), lookup, mask_term, reorder)
    kept_layers = (kept_first, kept_second)
    layer_masks = (None, mask_term)
    layer_orders = (None, reorder)
    grad_now = cotangent
    finished = []
    for layer_index in (1, 0):
        grad_now, weight_grads, small_grads, norm_grads = backward_layer(
            grad_now,
            kept_layers[layer_index],
            weights_of(layer_index),
            lookup,
            layer_masks[layer_index],
            layer_orders[layer_index],
        )
        d_qkv, d_proj, d_fc1, d_fc2 = weight_grads
        d_bias_qv, d_table, d_bias_fc1 = small_grads
        shards = (d_qkv[None], d_proj[None], d_fc1[None], d_fc2[None])
        finished.append((shards, (d_bias_qv[None], d_table[None], d_bias_fc1[None], norm_grads[None])))
    later_layer = finished[0]
    earlier_layer = finished[1]
    joined_qkv, joined_proj, joined_fc1, joined_fc2 = jax.tree.map(
        join_two, earlier_layer[0], later_layer[0]
    )
    smalls = jax.tree.map(join_two, earlier_layer[1], later_layer[1])
    joined_qkv, joined_proj, joined_fc1, joined_fc2 = (
        scatter_both(joined_qkv, 1, 3),
        scatter_both(joined_proj, 2, 1),
        scatter_both(joined_fc1, 1, 2),
        scatter_both(joined_fc2, 2, 1),
    )
    small_qv, small_table, small_fc1, small_norms = lax.psum(smalls, ("dp", "tensor"))
    dp_at, tensor_at = lax.axis_index("dp"), lax.axis_index("tensor")

    def own_part(values, at, size, dim):
        return lax.dynamic_slice_in_dim(values, at * size, size, axis=dim)

    d_bias_qv = own_part(small_qv, tensor_at, b_qv.shape[2], 2)
    d_table = own_part(small_table, tensor_at, bias_table.shape[2], 2)
    d_bias_fc1 = own_part(small_fc1, tensor_at, b_fc1.shape[1], 1)
    joined_norms = own_part(small_norms, dp_at, norm_params.shape[2], 2)
    return (
        second_out,
        grad_now,
        joined_qkv,
        d_bias_qv,
        d_table,
        joined_proj,
        joined_fc1,
        d_bias_fc1,
        joined_fc2,
        joined_norms,
    )


def solution(mesh):
    in_specs = (
        P(("dp", "tensor"), None),
        P(("dp", "tensor"), None),
        P(None, "dp", None, "tensor"),
        P(None, None, "tensor"),
        P(None, None, "tensor"),
        P(None, "tensor", "dp"),
        P(None, "dp", "tensor"),
        P(None, "tensor"),
        P(None, "tensor", "dp"),
        P(None, None, "dp"),
        P(),
        P(),
        P(),
    )
    out_specs = (
        P(("dp", "tensor"), None),
        P(("dp", "tensor"), None),
        P(None, "dp", None, "tensor"),
        P(None, None, "tensor"),
        P(None, None, "tensor"),
        P(None, "tensor", "dp"),
        P(None, "dp", "tensor"),
        P(None, "tensor"),
        P(None, "tensor", "dp"),
        P(None, None, "dp"),
    )
    return jax.shard_map(body, mesh=mesh, in_specs=in_specs, out_specs=out_specs, check_vma=False)
```

```python
import functools

import jax
import jax.numpy as jnp
from jax import lax
from jax.experimental import pallas as pl
from jax.experimental.pallas import tpu as pltpu
from jax.sharding import PartitionSpec as P

D = 512
HEAD_DIM = 32
WTOK = 49
ITOK = 196
NWIN = 4
RELS = 169
WROW = 56
QLANE = 64
IROW = NWIN * WROW

EPS = 1e-05
MASKED = -100.0
PADDED = -1e30
ROOT_HALF = 0.7071067811865476
ROOT_TWO_PI = 2.5066282746310002
SCALE = HEAD_DIM ** (-0.5)
full_precision = lax.Precision.HIGHEST
f32 = jnp.float32
bf16 = jnp.bfloat16


def dot_nn(a, b):
    return lax.dot_general(a, b, (((1,), (0,)), ((), ())), preferred_element_type=f32)


def dot_nt(a, b):
    return lax.dot_general(a, b, (((1,), (1,)), ((), ())), preferred_element_type=f32)


def dot_tn(a, b):
    return lax.dot_general(a, b, (((0,), (0,)), ((), ())), preferred_element_type=f32)


def normed_rows(hidden):
    centred = hidden - jnp.mean(hidden, axis=-1, keepdims=True)
    inv_std = lax.rsqrt(jnp.mean(centred * centred, axis=-1, keepdims=True) + EPS)
    return centred * inv_std, inv_std


def norm_back(scaled, normed, inv_std):
    return inv_std * (
        scaled
        - jnp.mean(scaled, axis=-1, keepdims=True)
        - normed * jnp.mean(scaled * normed, axis=-1, keepdims=True)
    )


def by_image(matrix, rows):
    count = rows.shape[0] // IROW
    parts = [
        dot_nn(matrix, rows[i * IROW : (i + 1) * IROW]).astype(bf16) for i in range(count)
    ]
    return jnp.concatenate(parts, axis=0)


def head_masks(heads):
    width = heads * HEAD_DIM
    lane = lax.broadcasted_iota(jnp.int32, (QLANE, width), 1) // HEAD_DIM
    row = lax.broadcasted_iota(jnp.int32, (QLANE, width), 0)
    return [jnp.where((lane == j) & (row < WTOK), 1.0, 0.0).astype(bf16) for j in range(heads)]


def spread_heads(rows, masks):
    return jnp.concatenate([rows * mask for mask in masks], axis=0)


def own_lanes(product, heads):
    lane = lax.broadcasted_iota(jnp.int32, (WROW, heads * HEAD_DIM), 1) // HEAD_DIM
    total = product[:WROW]
    for j in range(1, heads):
        total = jnp.where(lane == j, product[j * QLANE : j * QLANE + WROW], total)
    return total


def place_weight(me_ref, own_ref, other_ref, out_ref):
    half, _, block, _ = own_ref.shape
    near = me_ref[0] & 1
    for p in range(half):
        at = p ^ (me_ref[0] >> 1)
        first = pl.multiple_of((2 * p + near) * block, block)
        second = pl.multiple_of((2 * p + 1 - near) * block, block)
        out_ref[pl.ds(first, block), :] = own_ref[at, 0]
        out_ref[pl.ds(second, block), :] = other_ref[at, 0]


def place_grads(me_ref, grad_ref, keep_ref, send_ref, offset):
    half = keep_ref.shape[0]
    block = grad_ref.shape[0] // (2 * half)
    near = me_ref[0] & 1
    for p in range(half):
        at = p ^ (me_ref[0] >> 1)
        first = pl.multiple_of((2 * p + near) * block, block)
        second = pl.multiple_of((2 * p + 1 - near) * block, block)
        keep_ref[at, 0, offset : offset + block, :] = grad_ref[pl.ds(first, block), :]
        send_ref[at, 0, offset : offset + block, :] = grad_ref[pl.ds(second, block), :]


def attn_forward(heads, windows, shifted, me_ref, *refs):
    if shifted:
        mask_ref, perm_ref, back_ref = refs[:3]
        refs = refs[3:]
    h_ref, own_ref, other_ref, norm_ref, bqv_ref, bias_ref = refs[:6]
    h2_ref, ap_ref, qkv_ref, lse_ref, ou_ref, qkv_s, o_s, at_s = refs[6:]
    rows = h_ref.shape[0]
    width = heads * HEAD_DIM

    @pl.when(pl.program_id(0) == 0)
    def _():
        hidden = h_ref[...]
        normed, _ = normed_rows(hidden)
        ap = (normed * norm_ref[0:1] + norm_ref[1:2]).astype(bf16)
        if shifted:
            ap = by_image(perm_ref[...], ap)
        ap_ref[...] = ap
        h2_ref[...] = hidden + norm_ref[2:3]

    place_weight(me_ref, own_ref, other_ref, at_s)
    qkv = dot_nn(ap_ref[...], at_s[:, : 3 * width])
    query = (qkv[:, :width] + bqv_ref[0, 0:1]) * SCALE
    value = qkv[:, 2 * width :] + bqv_ref[0, 1:2]
    qkv = jnp.concatenate([query, qkv[:, width : 2 * width], value], axis=1)
    qkv_ref[...] = qkv.astype(bf16)
    qkv_s[:rows] = qkv
    masks = head_masks(heads)
    for w in range(windows):
        r0 = w * WROW
        query = spread_heads(qkv_s[r0 : r0 + QLANE, :width].astype(bf16), masks)
        key = qkv_s[r0 : r0 + WROW, width : 2 * width].astype(bf16)
        value = qkv_s[r0 : r0 + WROW, 2 * width :].astype(bf16)
        scores = dot_nt(key, query) + bias_ref[0]
        if shifted:
            scores = scores + mask_ref[w % NWIN]
        peak = jnp.max(scores, axis=0, keepdims=True)
        weights = jnp.exp(scores - peak)
        total = jnp.sum(weights, axis=0, keepdims=True)
        lse_ref[0, w : w + 1, :] = peak + jnp.log(total)
        weights = (weights * (1.0 / total)).astype(bf16)
        o_s[r0 : r0 + WROW, :] = own_lanes(dot_tn(weights, value), heads)
    ou = o_s[...].astype(bf16)
    if shifted:
        ou = by_image(back_ref[...], ou)
    ou_ref[...] = ou
    h2_ref[...] += dot_nt(ou, at_s[:, 3 * width :])


def mlp_forward(
    me_ref, h_ref, f1_own, f1_other, f2_own, f2_other, b1_ref, norm_ref,
    out_ref, act_ref, slope_ref, c_s, f1_s, f2_s,
):
    @pl.when(pl.program_id(0) == 0)
    def _():
        hidden = h_ref[...]
        normed, _ = normed_rows(hidden)
        c_s[...] = (normed * norm_ref[3:4] + norm_ref[4:5]).astype(bf16)
        out_ref[...] = hidden + norm_ref[5:6]

    place_weight(me_ref, f1_own, f1_other, f1_s)
    place_weight(me_ref, f2_own, f2_other, f2_s)
    pre = dot_nn(c_s[...], f1_s[...]) + b1_ref[0]
    phi = 0.5 * (1.0 + lax.erf(pre * ROOT_HALF))
    act = (pre * phi).astype(bf16)
    act_ref[...] = act
    slope_ref[...] = (phi + pre * jnp.exp(-0.5 * pre * pre) * (1.0 / ROOT_TWO_PI)).astype(bf16)
    out_ref[...] += dot_nt(act, f2_s[...])


def mlp_backward(
    me_ref, gh_ref, h_ref, act_ref, slope_ref, f1_own, f1_other, f2_own, f2_other, norm_ref,
    keep_ref, send_ref, db1_ref, dh2_ref, dnorm_ref, gz_s, gzt_s, ct_s, gc_s, f1_s, f2_s, df1_s, df2_s,
):
    step = pl.program_id(0)

    @pl.when(step == 0)
    def _():
        gz = gh_ref[...].astype(bf16)
        gz_s[...] = gz
        gzt_s[...] = jnp.transpose(gz)
        normed, _ = normed_rows(h_ref[...])
        ct_s[...] = jnp.transpose((normed * norm_ref[3:4] + norm_ref[4:5]).astype(bf16))

    place_weight(me_ref, f1_own, f1_other, f1_s)
    place_weight(me_ref, f2_own, f2_other, f2_s)
    df2_s[...] = dot_nn(gzt_s[...], act_ref[...]).astype(bf16)
    d_pre = dot_nn(gz_s[...], f2_s[...]) * slope_ref[...].astype(f32)
    db1_ref[0] = jnp.sum(d_pre, axis=0, keepdims=True)
    gu = d_pre.astype(bf16)
    df1_s[...] = dot_nn(ct_s[...], gu).astype(bf16)
    part = dot_nt(gu, f1_s[...])
    place_grads(me_ref, df1_s, keep_ref, send_ref, 0)
    place_grads(me_ref, df2_s, keep_ref, send_ref, keep_ref.shape[2] // 2)

    @pl.when(step == 0)
    def _():
        gc_s[...] = part

    @pl.when(step > 0)
    def _():
        gc_s[...] += part

    @pl.when(step == pl.num_programs(0) - 1)
    def _():
        gc = gc_s[...]
        gh = gh_ref[...]
        normed, inv_std = normed_rows(h_ref[...])
        dh2 = gh + norm_back(gc * norm_ref[3:4], normed, inv_std)
        dh2_ref[...] = dh2
        dnorm_ref[0:1] = jnp.sum(dh2, axis=0, keepdims=True)
        dnorm_ref[1:2] = jnp.sum(gc * normed, axis=0, keepdims=True)
        dnorm_ref[2:3] = jnp.sum(gc, axis=0, keepdims=True)
        dnorm_ref[3:4] = jnp.sum(gh, axis=0, keepdims=True)


def attn_backward(heads, windows, shifted, me_ref, *refs):
    if shifted:
        mask_ref, perm_ref, back_ref = refs[:3]
        refs = refs[3:]
    (
        dh2_ref, h_ref, ap_ref, qkv_ref, lse_ref, ou_ref, own_ref, other_ref, norm_ref, bias_ref,
        keep_ref, send_ref, dbqv_ref, dsum_ref, dh_ref, dnorm_ref,
        gy_s, gyt_s, apt_s, gn_s, qkv_s, go_s, gq_s, at_s, dat_s,
    ) = refs
    step = pl.program_id(0)
    rows = h_ref.shape[0]
    width = heads * HEAD_DIM

    @pl.when(step == 0)
    def _():
        gy = dh2_ref[...].astype(bf16)
        gy_s[...] = gy
        gyt_s[...] = jnp.transpose(gy)
        apt_s[...] = jnp.transpose(ap_ref[...])

    place_weight(me_ref, own_ref, other_ref, at_s)
    dat_s[:, 3 * width :] = dot_nn(gyt_s[...], ou_ref[...]).astype(bf16)
    go = dot_nn(gy_s[...], at_s[:, 3 * width :]).astype(bf16)
    if shifted:
        go = by_image(perm_ref[...], go)
    go_s[:rows] = go.astype(f32)
    qkv_s[:rows] = qkv_ref[...].astype(f32)
    masks = head_masks(heads)
    total = None
    for w in range(windows):
        r0 = w * WROW
        query = spread_heads(qkv_s[r0 : r0 + QLANE, :width].astype(bf16), masks)
        grad = spread_heads(go_s[r0 : r0 + QLANE].astype(bf16), masks)
        key = qkv_s[r0 : r0 + WROW, width : 2 * width].astype(bf16)
        value = qkv_s[r0 : r0 + WROW, 2 * width :].astype(bf16)
        scores = dot_nt(key, query) + bias_ref[0]
        if shifted:
            scores = scores + mask_ref[w % NWIN]
        exact = jnp.exp(scores - lse_ref[0, w : w + 1, :])
        weighed = exact * dot_nt(value, grad)
        d_scores = weighed - exact * jnp.sum(weighed, axis=0, keepdims=True)
        total = d_scores if w == 0 else total + d_scores
        rounded = d_scores.astype(bf16)
        gq_s[r0 : r0 + WROW, :width] = own_lanes(dot_tn(rounded, key), heads) * SCALE
        gq_s[r0 : r0 + WROW, width : 2 * width] = dot_nn(rounded, query)
        gq_s[r0 : r0 + WROW, 2 * width :] = dot_nn(exact.astype(bf16), grad)
    dsum_ref[0] = total
    dbqv_ref[0, 0:1] = jnp.sum(gq_s[:, :width], axis=0, keepdims=True)
    dbqv_ref[0, 1:2] = jnp.sum(gq_s[:, 2 * width :], axis=0, keepdims=True)
    gq = gq_s[...].astype(bf16)
    dat_s[:, : 3 * width] = dot_nn(apt_s[...], gq).astype(bf16)
    place_grads(me_ref, dat_s, keep_ref, send_ref, 0)
    if shifted:
        gq = by_image(back_ref[...], gq)
    part = dot_nt(gq, at_s[:, : 3 * width])

    @pl.when(step == 0)
    def _():
        gn_s[...] = part

    @pl.when(step > 0)
    def _():
        gn_s[...] += part

    @pl.when(step == pl.num_programs(0) - 1)
    def _():
        gn = gn_s[...]
        normed, inv_std = normed_rows(h_ref[...])
        dh_ref[...] = dh2_ref[...] + norm_back(gn * norm_ref[0:1], normed, inv_std)
        dnorm_ref[0:1] = jnp.sum(gn * normed, axis=0, keepdims=True)
        dnorm_ref[1:2] = jnp.sum(gn, axis=0, keepdims=True)


def whole(shape):
    return pl.BlockSpec(shape, lambda t, me: (0,) * len(shape))


def slab(shape, dim):
    return pl.BlockSpec(shape, lambda t, me: tuple(t if i == dim else 0 for i in range(len(shape))))


def weight_slab(half, block, columns, row):
    return pl.BlockSpec((half, 1, block, columns), lambda t, me: (0, t ^ me[1], row, 0))


def sds(shape, dtype):
    return jax.ShapeDtypeStruct(shape, dtype)


def call(kernel, name, groups, me, args, specs, outs, out_specs, scratch):
    return pl.pallas_call(
        kernel,
        grid_spec=pltpu.PrefetchScalarGridSpec(
            num_scalar_prefetch=1, grid=(groups,), in_specs=specs, out_specs=out_specs,
            scratch_shapes=[pltpu.VMEM(shape, dtype) for shape, dtype in scratch],
        ),
        out_shape=outs,
        name=name,
    )(me, *args)


def run_attn_forward(me, hidden, pack, norm_rows, bqv, bias, shift, sizes):
    rows, groups, heads, windows = sizes
    width = heads * HEAD_DIM
    own, other = pack
    half = own.shape[0]
    slab_of = weight_slab(half, D // (2 * half), 4 * width, 0)
    args = [*shift, hidden, own, other, norm_rows, bqv, bias]
    specs = [whole(x.shape) for x in shift] + [
        whole((rows, D)), slab_of, slab_of, whole(norm_rows.shape),
        slab((1,) + bqv.shape[1:], 0), slab((1,) + bias.shape[1:], 0),
    ]
    outs = [
        sds((rows, D), f32), sds((rows, D), bf16), sds((rows, 3 * D), bf16),
        sds((groups, windows, heads * QLANE), f32), sds((rows, D), bf16),
    ]
    out_specs = [
        whole((rows, D)), whole((rows, D)), slab((rows, 3 * width), 1),
        slab((1, windows, heads * QLANE), 0), slab((rows, width), 1),
    ]
    scratch = [((rows + 8, 3 * width), f32), ((rows, width), f32), ((D, 4 * width), bf16)]
    kernel = functools.partial(attn_forward, heads, windows, len(shift) > 0)
    return call(kernel, "attn_forward", groups, me, args, specs, outs, out_specs, scratch)


def run_mlp_forward(me, hidden, pack, b1, norm_rows, sizes):
    rows, groups, _, _ = sizes
    own, other = pack
    hid = b1.shape[-1]
    half = own.shape[0]
    f1, f2 = (weight_slab(half, D // (2 * half), hid, row) for row in (1, 2))
    args = [hidden, own, other, own, other, b1, norm_rows]
    specs = [whole((rows, D)), f1, f1, f2, f2, slab((1, 1, hid), 0), whole(norm_rows.shape)]
    outs = [sds((rows, D), f32), sds((rows, groups * hid), bf16), sds((rows, groups * hid), bf16)]
    out_specs = [whole((rows, D)), slab((rows, hid), 1), slab((rows, hid), 1)]
    scratch = [((rows, D), bf16), ((D, hid), bf16), ((D, hid), bf16)]
    return call(mlp_forward, "mlp_forward", groups, me, args, specs, outs, out_specs, scratch)


def run_mlp_backward(me, gh, hidden, act, slope, pack, norm_rows, sizes):
    rows, groups, _, _ = sizes
    own, other = pack
    hid = own.shape[-1]
    half = own.shape[0]
    block = D // (2 * half)
    f1, f2 = (weight_slab(half, block, hid, row) for row in (1, 2))
    args = [gh, hidden, act, slope, own, other, own, other, norm_rows]
    specs = [
        whole((rows, D)), whole((rows, D)), slab((rows, hid), 1), slab((rows, hid), 1),
        f1, f1, f2, f2, whole(norm_rows.shape),
    ]
    grads = sds((half, groups, 2 * block, hid), bf16)
    grads_slab = weight_slab(half, 2 * block, hid, 0)
    outs = [grads, grads, sds((groups, 1, hid), f32), sds((rows, D), f32), sds((8, D), f32)]
    out_specs = [grads_slab, grads_slab, slab((1, 1, hid), 0), whole((rows, D)), whole((8, D))]
    scratch = [
        ((rows, D), bf16), ((D, rows), bf16), ((D, rows), bf16), ((rows, D), f32),
        ((D, hid), bf16), ((D, hid), bf16), ((D, hid), bf16), ((D, hid), bf16),
    ]
    return call(mlp_backward, "mlp_backward", groups, me, args, specs, outs, out_specs, scratch)


def run_attn_backward(me, dh2, hidden, kept, pack, norm_rows, bias, shift, sizes):
    rows, groups, heads, windows = sizes
    width = heads * HEAD_DIM
    ap, qkv, lse, ou = kept
    own, other = pack
    half = own.shape[0]
    block = D // (2 * half)
    slab_of = weight_slab(half, block, 4 * width, 0)
    args = [*shift, dh2, hidden, ap, qkv, lse, ou, own, other, norm_rows, bias]
    specs = [whole(x.shape) for x in shift] + [
        whole((rows, D)), whole((rows, D)), whole((rows, D)), slab((rows, 3 * width), 1),
        slab((1,) + lse.shape[1:], 0), slab((rows, width), 1), slab_of, slab_of,
        whole(norm_rows.shape), slab((1,) + bias.shape[1:], 0),
    ]
    grads = sds((half, groups, block, 4 * width), bf16)
    outs = [
        grads, grads, sds((groups, 2, width), f32), sds((groups, WROW, heads * QLANE), f32),
        sds((rows, D), f32), sds((8, D), f32),
    ]
    out_specs = [
        slab_of, slab_of, slab((1, 2, width), 0), slab((1, WROW, heads * QLANE), 0),
        whole((rows, D)), whole((8, D)),
    ]
    scratch = [
        ((rows, D), bf16), ((D, rows), bf16), ((D, rows), bf16), ((rows, D), f32),
        ((rows + 8, 3 * width), f32), ((rows + 8, width), f32), ((rows, 3 * width), f32),
        ((D, 4 * width), bf16), ((D, 4 * width), bf16),
    ]
    kernel = functools.partial(attn_backward, heads, windows, len(shift) > 0)
    return call(kernel, "attn_backward", groups, me, args, specs, outs, out_specs, scratch)


def to_window_rows(tokens):
    windows = tokens.reshape(-1, WTOK, tokens.shape[-1])
    return jnp.pad(windows, ((0, 0), (0, WROW - WTOK), (0, 0))).reshape(-1, tokens.shape[-1])


def from_window_rows(rows):
    return rows.reshape(-1, WROW, rows.shape[-1])[:, :WTOK].reshape(-1, rows.shape[-1])


AXES = ("dp", "tensor")


def xor_send(values, dp_bits, tensor_bits):
    n_dp, n_tensor = lax.axis_size("dp"), lax.axis_size("tensor")
    pairs = [
        (d * n_tensor + t, (d ^ dp_bits) * n_tensor + (t ^ tensor_bits))
        for d in range(n_dp)
        for t in range(n_tensor)
    ]
    return lax.ppermute(values, AXES, pairs)


def xor_order(values, axis, index):
    return jnp.take(values, jnp.arange(values.shape[axis], dtype=jnp.int32) ^ index, axis=axis)


def on_small_slice():
    return lax.axis_size("dp") == 8 and lax.axis_size("tensor") == 4


def gather_tensor(shard):
    if on_small_slice():
        return jnp.stack([shard] + [xor_send(shard, 0, r) for r in (1, 2, 3)])
    gathered = lax.all_gather(shard, "tensor", axis=0, tiled=False)
    return xor_order(gathered, 0, lax.axis_index("tensor"))


def gather_dp(column):
    if on_small_slice():
        cut = column.shape[1] // 2
        from_x = xor_send(column, 2, 0)
        from_y = xor_send(column, 4, 0)
        far = [xor_send(from_x[:, :cut], 4, 0), xor_send(from_y[:, cut:], 2, 0)]
        own = jnp.stack([column, from_x, from_y, jnp.concatenate(far, axis=1)])
        return own, xor_send(own, 1, 0)
    gathered = lax.all_gather(column, "dp", axis=0, tiled=False)
    gathered = xor_order(gathered, 0, lax.axis_index("dp"))
    return gathered[0::2], gathered[1::2]


def scatter_sum(pairs):
    if on_small_slice():
        pairs = [(keep, xor_send(give, 1, 0)) for keep, give in pairs]

        def total(at):
            parts = [keep[at].astype(f32) + got[at].astype(f32) for keep, got in pairs]
            return jnp.concatenate(parts, axis=1) if len(parts) > 1 else parts[0]

        far = total(3).astype(bf16)
        cut = far.shape[1] // 2
        to_y = xor_send(far[:, :cut], 4, 0).astype(f32)
        to_x = xor_send(far[:, cut:], 2, 0).astype(f32)
        side = total(1)
        side = jnp.concatenate([side[:, :cut] + to_y, side[:, cut:]], axis=1)
        from_x = xor_send(side.astype(bf16), 2, 0).astype(f32)
        side = total(2)
        side = jnp.concatenate([side[:, :cut], side[:, cut:] + to_x], axis=1)
        from_y = xor_send(side.astype(bf16), 4, 0).astype(f32)
        column = total(0) + from_x + from_y
        sends = column.astype(bf16)
        got = [xor_send(sends[r], 0, r).astype(f32) for r in (1, 2, 3)]
        return column[0] + got[0] + got[1] + got[2]
    keep = jnp.concatenate([pair[0] for pair in pairs], axis=2)
    give = jnp.concatenate([pair[1] for pair in pairs], axis=2)
    blocks = jnp.stack([keep, give], axis=1).reshape((-1,) + keep.shape[1:])
    blocks = xor_order(blocks, 0, lax.axis_index("dp"))
    blocks = xor_order(blocks, 1, lax.axis_index("tensor"))
    part = lax.psum_scatter(blocks, "dp", scatter_dimension=0, tiled=False)
    return lax.psum_scatter(part, "tensor", scatter_dimension=0, tiled=False).astype(f32)


def sum_all(values):
    if on_small_slice():
        for dp_bits, tensor_bits in ((1, 0), (2, 0), (4, 0), (0, 1), (0, 2)):
            values = values + xor_send(values, dp_bits, tensor_bits)
        return values
    return lax.psum(values, AXES)


def body(
    block_input,
    cotangent,
    w_qkv,
    b_qv,
    bias_table,
    w_proj,
    w_fc1,
    b_fc1,
    w_fc2,
    norm_params,
    rel_index,
    shift_perm,
    shift_mask,
):
    n_dp, groups = lax.axis_size("dp"), lax.axis_size("tensor")
    dp_at, tensor_at = lax.axis_index("dp"), lax.axis_index("tensor")
    d_loc = w_qkv.shape[1]
    width = w_qkv.shape[3]
    hid = w_fc1.shape[2]
    heads = width // HEAD_DIM
    layers = w_qkv.shape[0]
    windows = block_input.shape[0] // WTOK
    rows = windows * WROW
    sizes = (rows, groups, heads, windows)

    me = jnp.stack([dp_at, tensor_at]).astype(jnp.int32)

    small = jnp.concatenate(
        [norm_params.reshape(-1), b_qv.reshape(-1), bias_table.reshape(-1), b_fc1.reshape(-1)]
    )
    n_small = small.shape[0]
    small_rows = -(-n_small // (16 * hid)) * 16
    small = jnp.pad(small, (0, small_rows * hid - n_small)).reshape(small_rows, hid)
    packs = []
    for layer in range(layers):
        attn = jnp.concatenate(
            [w_qkv[layer].reshape(d_loc, 3 * width), w_proj[layer].T], axis=1
        )
        share = [attn, w_fc1[layer], w_fc2[layer].T]
        share = jnp.concatenate(share + [small] if layer == 0 else share, axis=0)
        column = gather_tensor(share)
        if layer == 0:
            small_tensor = column[:, 3 * d_loc :].reshape(groups, -1)
        packs.append(gather_dp(column))
    small_dp = jnp.stack([part[:, 0, 3 * d_loc :] for part in packs[0]], axis=1)
    small_dp = xor_order(small_dp.reshape(n_dp, -1), 0, dp_at)
    small_tensor = xor_order(small_tensor, 0, tensor_at)

    ends = [0]
    for part in (norm_params, b_qv, bias_table, b_fc1):
        ends.append(ends[-1] + part.size)
    norm_all = small_dp[:, ends[0] : ends[1]].reshape((n_dp,) + norm_params.shape)
    norm_all = norm_all.transpose(1, 2, 0, 3).reshape(layers, 6, D).astype(f32)
    norm_all = jnp.pad(norm_all, ((0, 0), (0, 2), (0, 0)))
    bqv_all = small_tensor[:, ends[1] : ends[2]].reshape((groups,) + b_qv.shape).astype(f32)
    table_all = small_tensor[:, ends[2] : ends[3]].reshape((groups,) + bias_table.shape).astype(f32)
    b1_all = small_tensor[:, ends[3] : ends[4]].reshape((groups,) + b_fc1.shape).astype(f32)

    lookup = (rel_index.T.reshape(-1)[:, None] == jnp.arange(RELS, dtype=jnp.int32)).astype(f32)
    bias_all = jnp.einsum("cr,tlrh->ltch", lookup, table_all, precision=full_precision)
    bias_all = bias_all.reshape(layers, groups, WTOK, WTOK, heads).transpose(0, 1, 2, 4, 3)
    bias_all = jnp.pad(bias_all, ((0, 0), (0, 0), (0, 0), (0, 0), (0, QLANE - WTOK)))
    bias_all = bias_all.reshape(layers, groups, WTOK, heads * QLANE)
    bias_all = jnp.pad(
        bias_all, ((0, 0), (0, 0), (0, WROW - WTOK), (0, 0)), constant_values=PADDED
    )
    mask = (shift_mask.astype(f32) * MASKED).transpose(0, 2, 1)
    mask = jnp.pad(mask, ((0, 0), (0, WROW - WTOK), (0, QLANE - WTOK)))
    mask = jnp.tile(mask, (1, 1, heads))
    perm = shift_perm // WTOK * WROW + shift_perm % WTOK
    perm_rows = jnp.pad(perm.reshape(NWIN, WTOK), ((0, 0), (0, WROW - WTOK)), constant_values=-1)
    move = (perm_rows.reshape(-1)[:, None] == jnp.arange(IROW)[None, :]).astype(bf16)
    shift = (mask, move, move.T)

    hidden = to_window_rows(block_input)
    grad = to_window_rows(cotangent)

    kept = []
    for layer in range(layers):
        pack = packs[layer]
        bqv, b1 = bqv_all[:, layer], b1_all[:, layer][:, None]
        layer_shift = shift if layer == 1 else ()
        h2, ap, qkv, lse, ou = run_attn_forward(
            me, hidden, pack, norm_all[layer], bqv, bias_all[layer], layer_shift, sizes
        )
        out, act, slope = run_mlp_forward(me, h2, pack, b1, norm_all[layer], sizes)
        kept.append((hidden, h2, act, slope, (ap, qkv, lse, ou)))
        hidden = out
    block_output = from_window_rows(hidden)

    weight_grads = [None] * layers
    small_grads = [None] * layers
    for layer in (1, 0):
        pack = packs[layer]
        start, h2, act, slope, attn_kept = kept[layer]
        layer_shift = shift if layer == 1 else ()
        *mlp_grads, db1, dh2, dnorm_b = run_mlp_backward(
            me, grad, h2, act, slope, pack, norm_all[layer], sizes
        )
        *attn_grads, dbqv, dsum, grad, dnorm_a = run_attn_backward(
            me, dh2, start, attn_kept, pack, norm_all[layer], bias_all[layer], layer_shift, sizes
        )
        dscore = dsum[:, :WTOK].reshape(groups, WTOK, heads, QLANE)[..., :WTOK]
        dscore = dscore.transpose(1, 3, 0, 2).reshape(WTOK * WTOK, groups * heads)
        dtable = jnp.dot(lookup.T, dscore, precision=full_precision)
        dnorm = jnp.concatenate([dnorm_a[:2], dnorm_b[:4]], axis=0)
        weight_grads[layer] = scatter_sum([mlp_grads, attn_grads])
        small_grads[layer] = (dbqv.transpose(1, 0, 2).reshape(2, D), dtable, db1.reshape(-1), dnorm)
    small_parts = [jnp.stack(pair) for pair in zip(*small_grads, strict=True)]
    flat = jnp.concatenate([part.reshape(-1) for part in small_parts])
    flat = jnp.pad(flat, (0, -flat.shape[0] % (8 * D))).reshape(-1, D)
    flat = sum_all(flat).reshape(-1)
    small_sums = []
    for part in small_parts:
        small_sums.append(flat[: part.size].reshape(part.shape))
        flat = flat[part.size :]

    def own_part(values, at_index, size, dim):
        return lax.dynamic_slice_in_dim(values, at_index * size, size, axis=dim)

    d_bqv = own_part(small_sums[0], tensor_at, width, 2)
    d_table = own_part(small_sums[1], tensor_at, heads, 2)
    d_b1 = own_part(small_sums[2], tensor_at, hid, 1)
    d_norm = own_part(small_sums[3], dp_at, d_loc, 2)
    d_attn = [part[2 * d_loc :] for part in weight_grads]
    d_qkv = jnp.stack([x[:, : 3 * width].reshape(d_loc, 3, width) for x in d_attn])
    d_proj = jnp.stack([x[:, 3 * width :].T for x in d_attn])
    d_fc1 = jnp.stack([part[:d_loc] for part in weight_grads])
    d_fc2 = jnp.stack([part[d_loc : 2 * d_loc].T for part in weight_grads])
    return (
        block_output,
        from_window_rows(grad),
        d_qkv,
        d_bqv,
        d_table,
        d_proj,
        d_fc1,
        d_b1,
        d_fc2,
        d_norm,
    )


def solution(mesh):
    in_specs = (
        P(("dp", "tensor"), None),
        P(("dp", "tensor"), None),
        P(None, "dp", None, "tensor"),
        P(None, None, "tensor"),
        P(None, None, "tensor"),
        P(None, "tensor", "dp"),
        P(None, "dp", "tensor"),
        P(None, "tensor"),
        P(None, "tensor", "dp"),
        P(None, None, "dp"),
        P(),
        P(),
        P(),
    )
    out_specs = (
        P(("dp", "tensor"), None),
        P(("dp", "tensor"), None),
        P(None, "dp", None, "tensor"),
        P(None, None, "tensor"),
        P(None, None, "tensor"),
        P(None, "tensor", "dp"),
        P(None, "dp", "tensor"),
        P(None, "tensor"),
        P(None, "tensor", "dp"),
        P(None, None, "dp"),
    )
    return jax.shard_map(body, mesh=mesh, in_specs=in_specs, out_specs=out_specs, check_vma=False)
```

```python
import functools

import jax
import jax.numpy as jnp
from jax import lax
from jax.experimental import pallas as pl
from jax.experimental.pallas import tpu as pltpu
from jax.sharding import PartitionSpec as P

D = 512
HEAD_DIM = 32
WTOK = 49
ITOK = 196
NWIN = 4
RELS = 169
WROW = 56
QLANE = 64
IROW = NWIN * WROW

EPS = 1e-05
MASKED = -100.0
PADDED = -1e30
ROOT_HALF = 0.7071067811865476
ROOT_TWO_PI = 2.5066282746310002
SCALE = HEAD_DIM ** (-0.5)
full_precision = lax.Precision.HIGHEST
f32 = jnp.float32
bf16 = jnp.bfloat16


def dot_nn(a, b):
    return lax.dot_general(a, b, (((1,), (0,)), ((), ())), preferred_element_type=f32)


def dot_nt(a, b):
    return lax.dot_general(a, b, (((1,), (1,)), ((), ())), preferred_element_type=f32)


def dot_tn(a, b):
    return lax.dot_general(a, b, (((0,), (0,)), ((), ())), preferred_element_type=f32)


def normed_rows(hidden):
    centred = hidden - jnp.mean(hidden, axis=-1, keepdims=True)
    inv_std = lax.rsqrt(jnp.mean(centred * centred, axis=-1, keepdims=True) + EPS)
    return centred * inv_std, inv_std


def norm_back(scaled, normed, inv_std):
    return inv_std * (
        scaled
        - jnp.mean(scaled, axis=-1, keepdims=True)
        - normed * jnp.mean(scaled * normed, axis=-1, keepdims=True)
    )


def by_image(matrix, rows):
    count = rows.shape[0] // IROW
    parts = [
        dot_nn(matrix, rows[i * IROW : (i + 1) * IROW]).astype(bf16) for i in range(count)
    ]
    return jnp.concatenate(parts, axis=0)


def head_masks(heads):
    width = heads * HEAD_DIM
    lane = lax.broadcasted_iota(jnp.int32, (QLANE, width), 1) // HEAD_DIM
    row = lax.broadcasted_iota(jnp.int32, (QLANE, width), 0)
    return [jnp.where((lane == j) & (row < WTOK), 1.0, 0.0).astype(bf16) for j in range(heads)]


def spread_heads(rows, masks):
    return jnp.concatenate([rows * mask for mask in masks], axis=0)


def own_lanes(product, heads):
    lane = lax.broadcasted_iota(jnp.int32, (WROW, heads * HEAD_DIM), 1) // HEAD_DIM
    total = product[:WROW]
    for j in range(1, heads):
        total = jnp.where(lane == j, product[j * QLANE : j * QLANE + WROW], total)
    return total


def place_weight(me_ref, own_ref, other_ref, out_ref):
    half, _, block, _ = own_ref.shape
    near = me_ref[0] & 1
    for p in range(half):
        at = p ^ (me_ref[0] >> 1)
        first = pl.multiple_of((2 * p + near) * block, block)
        second = pl.multiple_of((2 * p + 1 - near) * block, block)
        out_ref[pl.ds(first, block), :] = own_ref[at, 0]
        out_ref[pl.ds(second, block), :] = other_ref[at, 0]


def place_grads(me_ref, grad_ref, keep_ref, send_ref, offset):
    half = keep_ref.shape[0]
    block = grad_ref.shape[0] // (2 * half)
    near = me_ref[0] & 1
    for p in range(half):
        at = p ^ (me_ref[0] >> 1)
        first = pl.multiple_of((2 * p + near) * block, block)
        second = pl.multiple_of((2 * p + 1 - near) * block, block)
        keep_ref[at, 0, offset : offset + block, :] = grad_ref[pl.ds(first, block), :]
        send_ref[at, 0, offset : offset + block, :] = grad_ref[pl.ds(second, block), :]


def spread_windows(src_ref, dst_ref):
    if src_ref.shape == dst_ref.shape:
        dst_ref[...] = src_ref[...]
        return
    dst_ref[...] = jnp.zeros_like(dst_ref)
    for w in range(src_ref.shape[0] // WTOK):
        dst_ref[w * WROW : w * WROW + WTOK, :] = src_ref[w * WTOK : (w + 1) * WTOK, :]


def pack_windows(src_ref, dst_ref):
    for w in range(dst_ref.shape[0] // WTOK):
        dst_ref[w * WTOK : (w + 1) * WTOK, :] = src_ref[w * WROW : w * WROW + WTOK, :]


def attn_forward(heads, windows, shifted, me_ref, *refs):
    if shifted:
        mask_ref, perm_ref, back_ref = refs[:3]
        refs = refs[3:]
    h_ref, own_ref, other_ref, norm_ref, bqv_ref, bias_ref = refs[:6]
    h2_ref, ap_ref, qkv_ref, lse_ref, ou_ref, qkv_s, o_s, at_s = refs[6:]
    rows = h2_ref.shape[0]
    width = heads * HEAD_DIM

    @pl.when(pl.program_id(0) == 0)
    def _():
        spread_windows(h_ref, h2_ref)
        hidden = h2_ref[...]
        normed, _ = normed_rows(hidden)
        ap = (normed * norm_ref[0:1] + norm_ref[1:2]).astype(bf16)
        if shifted:
            ap = by_image(perm_ref[...], ap)
        ap_ref[...] = ap
        h2_ref[...] = hidden + norm_ref[2:3]

    place_weight(me_ref, own_ref, other_ref, at_s)
    qkv = dot_nn(ap_ref[...], at_s[:, : 3 * width])
    query = (qkv[:, :width] + bqv_ref[0, 0:1]) * SCALE
    value = qkv[:, 2 * width :] + bqv_ref[0, 1:2]
    qkv = jnp.concatenate([query, qkv[:, width : 2 * width], value], axis=1)
    qkv_ref[...] = qkv.astype(bf16)
    qkv_s[:rows] = qkv
    masks = head_masks(heads)
    for w in range(windows):
        r0 = w * WROW
        query = spread_heads(qkv_s[r0 : r0 + QLANE, :width].astype(bf16), masks)
        key = qkv_s[r0 : r0 + WROW, width : 2 * width].astype(bf16)
        value = qkv_s[r0 : r0 + WROW, 2 * width :].astype(bf16)
        scores = dot_nt(key, query) + bias_ref[0]
        if shifted:
            scores = scores + mask_ref[w % NWIN]
        peak = jnp.max(scores, axis=0, keepdims=True)
        weights = jnp.exp(scores - peak)
        total = jnp.sum(weights, axis=0, keepdims=True)
        lse_ref[0, w : w + 1, :] = peak + jnp.log(total)
        weights = (weights * (1.0 / total)).astype(bf16)
        o_s[r0 : r0 + WROW, :] = own_lanes(dot_tn(weights, value), heads)
    ou = o_s[...].astype(bf16)
    if shifted:
        ou = by_image(back_ref[...], ou)
    ou_ref[...] = ou
    h2_ref[...] += dot_nt(ou, at_s[:, 3 * width :])


def mlp_forward(
    last, me_ref, h_ref, f1_own, f1_other, f2_own, f2_other, b1_ref, norm_ref,
    act_ref, slope_ref, result_ref, c_s, f1_s, f2_s, *total,
):
    out_ref = total[0] if last else result_ref

    @pl.when(pl.program_id(0) == 0)
    def _():
        hidden = h_ref[...]
        normed, _ = normed_rows(hidden)
        c_s[...] = (normed * norm_ref[3:4] + norm_ref[4:5]).astype(bf16)
        out_ref[...] = hidden + norm_ref[5:6]

    place_weight(me_ref, f1_own, f1_other, f1_s)
    place_weight(me_ref, f2_own, f2_other, f2_s)
    pre = dot_nn(c_s[...], f1_s[...]) + b1_ref[0]
    phi = 0.5 * (1.0 + lax.erf(pre * ROOT_HALF))
    act = (pre * phi).astype(bf16)
    act_ref[...] = act
    slope_ref[...] = (phi + pre * jnp.exp(-0.5 * pre * pre) * (1.0 / ROOT_TWO_PI)).astype(bf16)
    out_ref[...] += dot_nt(act, f2_s[...])
    if last:

        @pl.when(pl.program_id(0) == pl.num_programs(0) - 1)
        def _():
            pack_windows(out_ref, result_ref)


def mlp_backward(
    me_ref, gh_ref, h_ref, act_ref, slope_ref, f1_own, f1_other, f2_own, f2_other, norm_ref,
    keep_ref, send_ref, db1_ref, dh2_ref, dnorm_ref, gz_s, gzt_s, ct_s, gc_s, f1_s, f2_s, df1_s, df2_s,
):
    step = pl.program_id(0)

    @pl.when(step == 0)
    def _():
        spread_windows(gh_ref, dh2_ref)
        gz = dh2_ref[...].astype(bf16)
        gz_s[...] = gz
        gzt_s[...] = jnp.transpose(gz)
        normed, _ = normed_rows(h_ref[...])
        ct_s[...] = jnp.transpose((normed * norm_ref[3:4] + norm_ref[4:5]).astype(bf16))

    place_weight(me_ref, f1_own, f1_other, f1_s)
    place_weight(me_ref, f2_own, f2_other, f2_s)
    df2_s[...] = dot_nn(gzt_s[...], act_ref[...]).astype(bf16)
    d_pre = dot_nn(gz_s[...], f2_s[...]) * slope_ref[...].astype(f32)
    db1_ref[0] = jnp.sum(d_pre, axis=0, keepdims=True)
    gu = d_pre.astype(bf16)
    df1_s[...] = dot_nn(ct_s[...], gu).astype(bf16)
    part = dot_nt(gu, f1_s[...])
    place_grads(me_ref, df1_s, keep_ref, send_ref, 0)
    place_grads(me_ref, df2_s, keep_ref, send_ref, keep_ref.shape[2] // 2)

    @pl.when(step == 0)
    def _():
        gc_s[...] = part

    @pl.when(step > 0)
    def _():
        gc_s[...] += part

    @pl.when(step == pl.num_programs(0) - 1)
    def _():
        gc = gc_s[...]
        gh = dh2_ref[...]
        normed, inv_std = normed_rows(h_ref[...])
        dh2 = gh + norm_back(gc * norm_ref[3:4], normed, inv_std)
        dh2_ref[...] = dh2
        dnorm_ref[0:1] = jnp.sum(dh2, axis=0, keepdims=True)
        dnorm_ref[1:2] = jnp.sum(gc * normed, axis=0, keepdims=True)
        dnorm_ref[2:3] = jnp.sum(gc, axis=0, keepdims=True)
        dnorm_ref[3:4] = jnp.sum(gh, axis=0, keepdims=True)


def attn_backward(heads, windows, shifted, me_ref, *refs):
    if shifted:
        mask_ref, perm_ref, back_ref = refs[:3]
        refs = refs[3:]
    (
        dh2_ref, h_ref, ap_ref, qkv_ref, lse_ref, ou_ref, own_ref, other_ref, norm_ref, bias_ref,
        keep_ref, send_ref, dbqv_ref, dsum_ref, dh_ref, dnorm_ref,
        gy_s, gyt_s, apt_s, gn_s, qkv_s, go_s, gq_s, at_s, dat_s, *wide,
    ) = refs
    step = pl.program_id(0)
    rows = ap_ref.shape[0]
    width = heads * HEAD_DIM

    @pl.when(step == 0)
    def _():
        gy = dh2_ref[...].astype(bf16)
        gy_s[...] = gy
        gyt_s[...] = jnp.transpose(gy)
        apt_s[...] = jnp.transpose(ap_ref[...])

    place_weight(me_ref, own_ref, other_ref, at_s)
    dat_s[:, 3 * width :] = dot_nn(gyt_s[...], ou_ref[...]).astype(bf16)
    go = dot_nn(gy_s[...], at_s[:, 3 * width :]).astype(bf16)
    if shifted:
        go = by_image(perm_ref[...], go)
    go_s[:rows] = go.astype(f32)
    qkv_s[:rows] = qkv_ref[...].astype(f32)
    masks = head_masks(heads)
    total = None
    for w in range(windows):
        r0 = w * WROW
        query = spread_heads(qkv_s[r0 : r0 + QLANE, :width].astype(bf16), masks)
        grad = spread_heads(go_s[r0 : r0 + QLANE].astype(bf16), masks)
        key = qkv_s[r0 : r0 + WROW, width : 2 * width].astype(bf16)
        value = qkv_s[r0 : r0 + WROW, 2 * width :].astype(bf16)
        scores = dot_nt(key, query) + bias_ref[0]
        if shifted:
            scores = scores + mask_ref[w % NWIN]
        exact = jnp.exp(scores - lse_ref[0, w : w + 1, :])
        weighed = exact * dot_nt(value, grad)
        d_scores = weighed - exact * jnp.sum(weighed, axis=0, keepdims=True)
        total = d_scores if w == 0 else total + d_scores
        rounded = d_scores.astype(bf16)
        gq_s[r0 : r0 + WROW, :width] = own_lanes(dot_tn(rounded, key), heads) * SCALE
        gq_s[r0 : r0 + WROW, width : 2 * width] = dot_nn(rounded, query)
        gq_s[r0 : r0 + WROW, 2 * width :] = dot_nn(exact.astype(bf16), grad)
    dsum_ref[0] = total
    dbqv_ref[0, 0:1] = jnp.sum(gq_s[:, :width], axis=0, keepdims=True)
    dbqv_ref[0, 1:2] = jnp.sum(gq_s[:, 2 * width :], axis=0, keepdims=True)
    gq = gq_s[...].astype(bf16)
    dat_s[:, : 3 * width] = dot_nn(apt_s[...], gq).astype(bf16)
    place_grads(me_ref, dat_s, keep_ref, send_ref, 0)
    if shifted:
        gq = by_image(back_ref[...], gq)
    part = dot_nt(gq, at_s[:, : 3 * width])

    @pl.when(step == 0)
    def _():
        gn_s[...] = part

    @pl.when(step > 0)
    def _():
        gn_s[...] += part

    @pl.when(step == pl.num_programs(0) - 1)
    def _():
        gn = gn_s[...]
        if wide:
            spread_windows(h_ref, wide[0])
        normed, inv_std = normed_rows((wide[0] if wide else h_ref)[...])
        (wide[0] if wide else dh_ref)[...] = dh2_ref[...] + norm_back(
            gn * norm_ref[0:1], normed, inv_std
        )
        if wide:
            pack_windows(wide[0], dh_ref)
        dnorm_ref[0:1] = jnp.sum(gn * normed, axis=0, keepdims=True)
        dnorm_ref[1:2] = jnp.sum(gn, axis=0, keepdims=True)


def whole(shape):
    return pl.BlockSpec(shape, lambda t, me: (0,) * len(shape))


def slab(shape, dim):
    return pl.BlockSpec(shape, lambda t, me: tuple(t if i == dim else 0 for i in range(len(shape))))


def weight_slab(half, block, columns, row):
    return pl.BlockSpec((half, 1, block, columns), lambda t, me: (0, t ^ me[1], row, 0))


def sds(shape, dtype):
    return jax.ShapeDtypeStruct(shape, dtype)


def call(kernel, name, groups, me, args, specs, outs, out_specs, scratch, micros):
    moved = sum(x.size * x.dtype.itemsize for x in [*args, *outs])
    cost = pl.CostEstimate(flops=int(micros * 1e9), transcendentals=0, bytes_accessed=moved)
    return pl.pallas_call(
        kernel,
        grid_spec=pltpu.PrefetchScalarGridSpec(
            num_scalar_prefetch=1, grid=(groups,), in_specs=specs, out_specs=out_specs,
            scratch_shapes=[pltpu.VMEM(shape, dtype) for shape, dtype in scratch],
        ),
        out_shape=outs,
        cost_estimate=cost,
        name=name,
    )(me, *args)


def run_attn_forward(me, hidden, pack, norm_rows, bqv, bias, shift, sizes):
    rows, groups, heads, windows = sizes
    width = heads * HEAD_DIM
    own, other = pack
    half = own.shape[0]
    slab_of = weight_slab(half, D // (2 * half), 4 * width, 0)
    args = [*shift, hidden, own, other, norm_rows, bqv, bias]
    specs = [whole(x.shape) for x in shift] + [
        whole(hidden.shape), slab_of, slab_of, whole(norm_rows.shape),
        slab((1,) + bqv.shape[1:], 0), slab((1,) + bias.shape[1:], 0),
    ]
    outs = [
        sds((rows, D), f32), sds((rows, D), bf16), sds((rows, 3 * D), bf16),
        sds((groups, windows, heads * QLANE), f32), sds((rows, D), bf16),
    ]
    out_specs = [
        whole((rows, D)), whole((rows, D)), slab((rows, 3 * width), 1),
        slab((1, windows, heads * QLANE), 0), slab((rows, width), 1),
    ]
    scratch = [((rows + 8, 3 * width), f32), ((rows, width), f32), ((D, 4 * width), bf16)]
    kernel = functools.partial(attn_forward, heads, windows, len(shift) > 0)
    return call(kernel, "attn_forward", groups, me, args, specs, outs, out_specs, scratch, 8)


def run_mlp_forward(me, hidden, pack, b1, norm_rows, last, sizes):
    rows, groups, _, windows = sizes
    own, other = pack
    hid = b1.shape[-1]
    half = own.shape[0]
    f1, f2 = (weight_slab(half, D // (2 * half), hid, row) for row in (1, 2))
    args = [hidden, own, other, own, other, b1, norm_rows]
    specs = [whole((rows, D)), f1, f1, f2, f2, slab((1, 1, hid), 0), whole(norm_rows.shape)]
    result = (windows * WTOK if last else rows, D)
    outs = [sds((rows, groups * hid), bf16), sds((rows, groups * hid), bf16), sds(result, f32)]
    out_specs = [slab((rows, hid), 1), slab((rows, hid), 1), whole(result)]
    scratch = [((rows, D), bf16), ((D, hid), bf16), ((D, hid), bf16)]
    scratch += [((rows, D), f32)] if last else []
    return call(functools.partial(mlp_forward, last), "mlp_forward", groups, me, args, specs, outs, out_specs, scratch, 8)


def run_mlp_backward(me, gh, hidden, act, slope, pack, norm_rows, sizes):
    rows, groups, _, _ = sizes
    own, other = pack
    hid = own.shape[-1]
    half = own.shape[0]
    block = D // (2 * half)
    f1, f2 = (weight_slab(half, block, hid, row) for row in (1, 2))
    args = [gh, hidden, act, slope, own, other, own, other, norm_rows]
    specs = [
        whole(gh.shape), whole((rows, D)), slab((rows, hid), 1), slab((rows, hid), 1),
        f1, f1, f2, f2, whole(norm_rows.shape),
    ]
    grads = sds((half, groups, 2 * block, hid), bf16)
    grads_slab = weight_slab(half, 2 * block, hid, 0)
    outs = [grads, grads, sds((groups, 1, hid), f32), sds((rows, D), f32), sds((8, D), f32)]
    out_specs = [grads_slab, grads_slab, slab((1, 1, hid), 0), whole((rows, D)), whole((8, D))]
    scratch = [
        ((rows, D), bf16), ((D, rows), bf16), ((D, rows), bf16), ((rows, D), f32),
        ((D, hid), bf16), ((D, hid), bf16), ((D, hid), bf16), ((D, hid), bf16),
    ]
    return call(mlp_backward, "mlp_backward", groups, me, args, specs, outs, out_specs, scratch, 12)


def run_attn_backward(me, dh2, hidden, kept, pack, norm_rows, bias, shift, sizes):
    rows, groups, heads, windows = sizes
    width = heads * HEAD_DIM
    ap, qkv, lse, ou = kept
    own, other = pack
    half = own.shape[0]
    block = D // (2 * half)
    slab_of = weight_slab(half, block, 4 * width, 0)
    args = [*shift, dh2, hidden, ap, qkv, lse, ou, own, other, norm_rows, bias]
    specs = [whole(x.shape) for x in shift] + [
        whole((rows, D)), whole(hidden.shape), whole((rows, D)), slab((rows, 3 * width), 1),
        slab((1,) + lse.shape[1:], 0), slab((rows, width), 1), slab_of, slab_of,
        whole(norm_rows.shape), slab((1,) + bias.shape[1:], 0),
    ]
    grads = sds((half, groups, block, 4 * width), bf16)
    outs = [
        grads, grads, sds((groups, 2, width), f32), sds((groups, WROW, heads * QLANE), f32),
        sds(hidden.shape, f32), sds((8, D), f32),
    ]
    out_specs = [
        slab_of, slab_of, slab((1, 2, width), 0), slab((1, WROW, heads * QLANE), 0),
        whole(hidden.shape), whole((8, D)),
    ]
    scratch = [
        ((rows, D), bf16), ((D, rows), bf16), ((D, rows), bf16), ((rows, D), f32),
        ((rows + 8, 3 * width), f32), ((rows + 8, width), f32), ((rows, 3 * width), f32),
        ((D, 4 * width), bf16), ((D, 4 * width), bf16),
    ]
    scratch += [((rows, D), f32)] if hidden.shape[0] != rows else []
    kernel = functools.partial(attn_backward, heads, windows, len(shift) > 0)
    return call(kernel, "attn_backward", groups, me, args, specs, outs, out_specs, scratch, 19)


AXES = ("dp", "tensor")


def after(values, *others):
    return lax.optimization_barrier((values, *others))[0]


def xor_send(values, dp_bits, tensor_bits):
    n_dp, n_tensor = lax.axis_size("dp"), lax.axis_size("tensor")
    pairs = [
        (d * n_tensor + t, (d ^ dp_bits) * n_tensor + (t ^ tensor_bits))
        for d in range(n_dp)
        for t in range(n_tensor)
    ]
    return lax.ppermute(values, AXES, pairs)


def xor_order(values, axis, index):
    return jnp.take(values, jnp.arange(values.shape[axis], dtype=jnp.int32) ^ index, axis=axis)


def on_small_slice():
    return lax.axis_size("dp") == 8 and lax.axis_size("tensor") == 4


def gather_tensor(shard):
    if on_small_slice():
        return jnp.stack([shard] + [xor_send(shard, 0, r) for r in (1, 2, 3)])
    gathered = lax.all_gather(shard, "tensor", axis=0, tiled=False)
    return xor_order(gathered, 0, lax.axis_index("tensor"))


class Gather:
    def __init__(self, share, *then):
        self.column = gather_tensor(after(share, *then))

    def side_stage(self, *then):
        self.column = after(self.column, *then)
        self.from_x = xor_send(self.column, 2, 0)
        self.from_y = xor_send(self.column, 4, 0)

    def far_stage(self, *then):
        from_x, from_y = after(self.from_x, *then), after(self.from_y, *then)
        cut = self.column.shape[0] // 2
        self.far = (xor_send(from_x[:cut], 4, 0), xor_send(from_y[cut:], 2, 0))

    def pair_stage(self):
        far = jnp.concatenate(self.far, axis=0)
        own = jnp.stack([self.column, self.from_x, self.from_y, far])
        return own, xor_send(own, 1, 0)

    def whole(self):
        gathered = lax.all_gather(self.column, "dp", axis=0, tiled=False)
        gathered = xor_order(gathered, 0, lax.axis_index("dp"))
        return gathered[0::2], gathered[1::2]


def gather_small(values):
    if not on_small_slice():
        return lax.all_gather(values, "dp", axis=0, tiled=False)
    rows = values[None]
    for bits in (1, 2, 4):
        rows = jnp.concatenate([rows, xor_send(rows, bits, 0)], axis=0)
    return xor_order(rows, 0, lax.axis_index("dp"))


def add_far(*refs):
    *parts, first_ref, second_ref = refs
    half = first_ref.shape[0]
    row = 0
    for keep_ref, got_ref in zip(parts[::2], parts[1::2], strict=True):
        rows = slice(row, row + keep_ref.shape[2])
        total = (keep_ref[0].astype(f32) + got_ref[0].astype(f32)).astype(bf16)
        first_ref[:, rows] = total[:half]
        second_ref[:, rows] = total[half:]
        row = rows.stop


def add_side(*refs):
    *parts, to_y_ref, to_x_ref, side_x_ref, side_y_ref = refs
    first = 2 * pl.program_id(0) < pl.num_programs(0)
    row = 0
    for keep_x, got_x, keep_y, got_y in zip(*(parts[i::4] for i in range(4)), strict=True):
        rows = slice(row, row + keep_x.shape[2])
        more_x = jnp.where(first, to_y_ref[0, rows].astype(f32), 0.0)
        more_y = jnp.where(first, 0.0, to_x_ref[0, rows].astype(f32))
        side_x_ref[0, rows] = (keep_x[0, 0].astype(f32) + got_x[0, 0].astype(f32) + more_x).astype(bf16)
        side_y_ref[0, rows] = (keep_y[0, 0].astype(f32) + got_y[0, 0].astype(f32) + more_y).astype(bf16)
        row = rows.stop


def add_column(*refs):
    *parts, from_x_ref, from_y_ref, own_ref, send_1, send_2, send_3 = refs
    row = 0
    for keep_ref, got_ref in zip(parts[::2], parts[1::2], strict=True):
        rows = slice(row, row + keep_ref.shape[2])
        for at, out_ref in enumerate((own_ref, send_1, send_2, send_3)):
            total = keep_ref[0, at].astype(f32) + got_ref[0, at].astype(f32)
            total += from_x_ref[at, rows].astype(f32) + from_y_ref[at, rows].astype(f32)
            out_ref[rows] = total.astype(out_ref.dtype)
        row = rows.stop


def finish(*refs):
    *parts, qkv_ref, proj_ref, fc1_ref, fc2_ref = refs
    block, width = proj_ref.shape[1:]
    for layer in range(qkv_ref.shape[0]):
        own, *got = parts[4 * layer : 4 * layer + 4]
        total = own[...] + got[0][...].astype(f32) + got[1][...].astype(f32) + got[2][...].astype(f32)
        fc1_ref[layer] = total[:block]
        fc2_ref[layer] = total[block : 2 * block]
        for i in range(3):
            qkv_ref[layer, i] = total[2 * block :, i * width : (i + 1) * width]
        proj_ref[layer] = total[2 * block :, 3 * width :]


def one_block(array, at):
    return pl.BlockSpec((1,) + array.shape[1:], lambda *_: (at,) + (0,) * (array.ndim - 1))


def tensor_block(array, at):
    shape = (1, 1) + array.shape[2:]
    return pl.BlockSpec(shape, lambda z: (at, z) + (0,) * (array.ndim - 2))


class Scatter:
    def __init__(self, keep, give):
        self.keep = [keep]
        self.give = [give]
        self.got = [xor_send(give, 1, 0)] if on_small_slice() else []

    def join(self, other):
        self.keep += other.keep
        self.give += other.give
        self.got += other.got

    def parts(self):
        return [x for pair in zip(self.keep, self.got, strict=True) for x in pair]

    def far_stage(self, *then):
        self.got = [after(got, *then) for got in self.got]
        parts = self.parts()
        _, count, _, columns = parts[0].shape
        self.rows = sum(x.shape[2] for x in self.keep)
        half = sds((count // 2, self.rows, columns), bf16)
        self.far = pl.pallas_call(
            add_far,
            grid=(1,),
            in_specs=[one_block(x, 3) for x in parts],
            out_specs=[pl.BlockSpec(half.shape, lambda i: (0, 0, 0))] * 2,
            out_shape=[half, half],
            name="add_far",
        )(*parts)
        self.to_y = xor_send(self.far[0], 4, 0)
        self.to_x = xor_send(self.far[1], 2, 0)
        return self.far

    def side_stage(self, *then):
        to_x, to_y = after(self.to_x, *then), after(self.to_y, *then)
        specs, args = [], []
        for keep, got in zip(self.keep, self.got, strict=True):
            args += [keep, got, keep, got]
            specs += [tensor_block(keep, 1), tensor_block(got, 1), tensor_block(keep, 2), tensor_block(got, 2)]
        count, columns = self.keep[0].shape[1], self.keep[0].shape[3]
        half = count // 2
        block = (1, self.rows, columns)
        specs += [
            pl.BlockSpec(block, lambda z: (jnp.minimum(z, half - 1), 0, 0)),
            pl.BlockSpec(block, lambda z: (jnp.maximum(z - half, 0), 0, 0)),
        ]
        side = sds((count, self.rows, columns), bf16)
        self.side = pl.pallas_call(
            add_side,
            grid=(count,),
            in_specs=specs,
            out_specs=[pl.BlockSpec(block, lambda z: (z, 0, 0))] * 2,
            out_shape=[side, side],
            name="add_side",
        )(*args, to_y, to_x)
        self.from_x = xor_send(self.side[0], 2, 0)
        self.from_y = xor_send(self.side[1], 4, 0)
        return self.side

    def column_stage(self, *then):
        from_x, from_y = after(self.from_x, *then), after(self.from_y, *then)
        parts = self.parts()
        columns = parts[0].shape[3]
        own, send = sds((self.rows, columns), f32), sds((self.rows, columns), bf16)
        flat = pl.BlockSpec(own.shape, lambda i: (0, 0))
        self.own, *self.sends = pl.pallas_call(
            add_column,
            grid=(1,),
            in_specs=[one_block(x, 0) for x in parts]
            + [pl.BlockSpec(from_x.shape, lambda i: (0, 0, 0))] * 2,
            out_specs=[flat] * 4,
            out_shape=[own, send, send, send],
            name="add_column",
        )(*parts, from_x, from_y)
        self.ends = [self.own] + [xor_send(x, 0, r) for r, x in zip((1, 2, 3), self.sends, strict=True)]
        return self.sends

    def whole(self):
        keep, give = (jnp.concatenate(x, axis=2) for x in (self.keep, self.give))
        blocks = jnp.stack([keep, give], axis=1).reshape((-1,) + keep.shape[1:])
        blocks = xor_order(blocks, 0, lax.axis_index("dp"))
        blocks = xor_order(blocks, 1, lax.axis_index("tensor"))
        part = lax.psum_scatter(blocks, "dp", scatter_dimension=0, tiled=False)
        part = lax.psum_scatter(part, "tensor", scatter_dimension=0, tiled=False)
        zero = jnp.zeros_like(part)
        self.ends = [part.astype(f32), zero, zero, zero]


def sum_over(values, *bits):
    for dp_bits, tensor_bits in bits:
        values = values + xor_send(values, dp_bits, tensor_bits)
    return values


def body(
    block_input,
    cotangent,
    w_qkv,
    b_qv,
    bias_table,
    w_proj,
    w_fc1,
    b_fc1,
    w_fc2,
    norm_params,
    rel_index,
    shift_perm,
    shift_mask,
):
    n_dp, groups = lax.axis_size("dp"), lax.axis_size("tensor")
    dp_at, tensor_at = lax.axis_index("dp"), lax.axis_index("tensor")
    d_loc = w_qkv.shape[1]
    width = w_qkv.shape[3]
    hid = w_fc1.shape[2]
    heads = width // HEAD_DIM
    layers = w_qkv.shape[0]
    windows = block_input.shape[0] // WTOK
    rows = windows * WROW
    sizes = (rows, groups, heads, windows)

    me = jnp.stack([dp_at, tensor_at]).astype(jnp.int32)

    norm_flat = norm_params.reshape(-1)
    norm_flat = jnp.pad(norm_flat, (0, -norm_flat.size % 2048)).reshape(-1, 128)
    norm_all = gather_small(norm_flat).reshape(n_dp, -1)[:, : norm_params.size]
    norm_all = norm_all.reshape((n_dp,) + norm_params.shape)
    norm_all = norm_all.transpose(1, 2, 0, 3).reshape(layers, 6, D).astype(f32)
    norm_all = jnp.pad(norm_all, ((0, 0), (0, 2), (0, 0)))

    small = jnp.concatenate([b_qv.reshape(-1), bias_table.reshape(-1), b_fc1.reshape(-1)])
    n_small = small.shape[0]
    small_rows = -(-n_small // (16 * hid)) * 16
    small = jnp.pad(small, (0, small_rows * hid - n_small)).reshape(small_rows, hid)
    shares = []
    for layer in range(layers):
        attn = jnp.concatenate(
            [w_qkv[layer].reshape(d_loc, 3 * width), w_proj[layer].T], axis=1
        )
        share = [attn, w_fc1[layer], w_fc2[layer].T]
        shares.append(jnp.concatenate(share + [small] if layer == 0 else share, axis=0))
    staged = on_small_slice()
    first = Gather(shares[0])
    small_tensor = first.column[:, 3 * d_loc :].reshape(groups, -1)
    second = Gather(shares[1], first.column)
    if staged:
        first.side_stage()
        first.far_stage(second.column)
        second.side_stage(*first.far)
        packs = [first.pair_stage(), None]
    else:
        packs = [first.whole(), second.whole()]
    small_tensor = xor_order(small_tensor, 0, tensor_at)

    ends = [0]
    for part in (b_qv, bias_table, b_fc1):
        ends.append(ends[-1] + part.size)
    bqv_all = small_tensor[:, ends[0] : ends[1]].reshape((groups,) + b_qv.shape).astype(f32)
    table_all = small_tensor[:, ends[1] : ends[2]].reshape((groups,) + bias_table.shape).astype(f32)
    b1_all = small_tensor[:, ends[2] : ends[3]].reshape((groups,) + b_fc1.shape).astype(f32)

    lookup = (rel_index.T.reshape(-1)[:, None] == jnp.arange(RELS, dtype=jnp.int32)).astype(f32)
    bias_all = jnp.einsum("cr,tlrh->ltch", lookup, table_all, precision=full_precision)
    bias_all = bias_all.reshape(layers, groups, WTOK, WTOK, heads).transpose(0, 1, 2, 4, 3)
    bias_all = jnp.pad(bias_all, ((0, 0), (0, 0), (0, 0), (0, 0), (0, QLANE - WTOK)))
    bias_all = bias_all.reshape(layers, groups, WTOK, heads * QLANE)
    bias_all = jnp.pad(
        bias_all, ((0, 0), (0, 0), (0, WROW - WTOK), (0, 0)), constant_values=PADDED
    )
    mask = (shift_mask.astype(f32) * MASKED).transpose(0, 2, 1)
    mask = jnp.pad(mask, ((0, 0), (0, WROW - WTOK), (0, QLANE - WTOK)))
    mask = jnp.tile(mask, (1, 1, heads))
    perm = shift_perm // WTOK * WROW + shift_perm % WTOK
    perm_rows = jnp.pad(perm.reshape(NWIN, WTOK), ((0, 0), (0, WROW - WTOK)), constant_values=-1)
    move = (perm_rows.reshape(-1)[:, None] == jnp.arange(IROW)[None, :]).astype(bf16)
    shift = (mask, move, move.T)

    hidden = block_input
    grad = cotangent

    def attn_layer(layer, hidden):
        return run_attn_forward(
            me, hidden, packs[layer], norm_all[layer], bqv_all[:, layer], bias_all[layer],
            shift if layer == 1 else (), sizes,
        )

    def mlp_layer(layer, h2):
        b1 = b1_all[:, layer][:, None]
        return run_mlp_forward(me, h2, packs[layer], b1, norm_all[layer], layer == 1, sizes)

    kept = [None, None]
    if staged:
        hidden = after(hidden, second.column)
    h2, *attn_kept = attn_layer(0, hidden)
    act, slope, out = mlp_layer(0, h2)
    kept[0] = (hidden, h2, act, slope, attn_kept)
    hidden = out
    if staged:
        second.far_stage(out)
        packs[1] = second.pair_stage()
    h2, *attn_kept = attn_layer(1, hidden)
    act, slope, out = mlp_layer(1, h2)
    kept[1] = (hidden, h2, act, slope, attn_kept)
    hidden = out
    block_output = hidden

    def mlp_grads(layer, grad):
        start, h2, act, slope, _ = kept[layer]
        keep, give, db1, dh2, dnorm = run_mlp_backward(
            me, grad, h2, act, slope, packs[layer], norm_all[layer], sizes
        )
        return Scatter(keep, give), dh2, (db1, dnorm)

    def attn_grads(layer, dh2):
        start, _, _, _, attn_kept = kept[layer]
        keep, give, dbqv, dsum, grad, dnorm = run_attn_backward(
            me, dh2, start, attn_kept, packs[layer], norm_all[layer], bias_all[layer],
            shift if layer == 1 else (), sizes,
        )
        return Scatter(keep, give), grad, (dbqv, dsum, dnorm)

    mlp_1, dh2, from_mlp_1 = mlp_grads(1, grad)
    attn_1, grad, from_attn_1 = attn_grads(1, dh2)
    mlp_1.join(attn_1)
    if staged:
        grad = after(grad, *mlp_1.far_stage(grad))
    mlp_0, dh2, from_mlp_0 = mlp_grads(0, grad)
    if staged:
        dh2 = after(dh2, *mlp_1.side_stage(dh2))
    attn_0, grad, from_attn_0 = attn_grads(0, dh2)
    mlp_0.join(attn_0)
    if staged:
        mlp_0.far_stage(grad)
        mlp_1.column_stage(*mlp_0.far)
        mlp_0.side_stage(*mlp_1.sends)
        mlp_0.column_stage()
    else:
        mlp_1.whole()
        mlp_0.whole()

    pairs = ((from_mlp_0, from_attn_0), (from_mlp_1, from_attn_1))
    db1 = jnp.stack([mlp_part[0].reshape(-1) for mlp_part, _ in pairs])
    dbqv = jnp.stack([attn_part[0] for _, attn_part in pairs])
    dsum = jnp.stack([attn_part[1] for _, attn_part in pairs])
    if staged:
        dsum = after(dsum, *mlp_0.side)
    dnorm = jnp.stack(
        [jnp.concatenate([attn[2][:2], mlp[1][:4]], axis=0) for mlp, attn in pairs]
    )
    dscore = dsum[:, :, :WTOK].reshape(layers, groups, WTOK, heads, QLANE)[..., :WTOK]
    dscore = dscore.transpose(2, 4, 0, 1, 3).reshape(WTOK * WTOK, layers * groups * heads)
    dtable = jnp.dot(lookup.T, dscore, precision=full_precision)
    dtable = dtable.reshape(RELS, layers, groups * heads).transpose(1, 0, 2)
    small_parts = [dbqv.transpose(0, 2, 1, 3).reshape(layers, 2, D), dtable, db1, dnorm]
    flat = jnp.concatenate([part.reshape(-1) for part in small_parts])
    flat = jnp.pad(flat, (0, -flat.shape[0] % (8 * D))).reshape(-1, D)
    if staged:
        flat = sum_over(flat, (0, 1), (0, 2))
        flat = sum_over(after(flat, *mlp_0.sends), (1, 0), (2, 0), (4, 0))
    else:
        flat = lax.psum(flat, AXES)
    flat = flat.reshape(-1)
    small_sums = []
    for part in small_parts:
        small_sums.append(flat[: part.size].reshape(part.shape))
        flat = flat[part.size :]

    def own_part(values, at_index, size, dim):
        return lax.dynamic_slice_in_dim(values, at_index * size, size, axis=dim)

    d_bqv = own_part(small_sums[0], tensor_at, width, 2)
    d_table = own_part(small_sums[1], tensor_at, heads, 2)
    d_b1 = own_part(small_sums[2], tensor_at, hid, 1)
    d_norm = own_part(small_sums[3], dp_at, d_loc, 2)
    shapes = [
        (layers, 3, d_loc, width), (layers, d_loc, width),
        (layers, d_loc, hid), (layers, d_loc, hid),
    ]
    d_qkv, d_proj, d_fc1, d_fc2 = pl.pallas_call(
        finish, out_shape=[sds(shape, f32) for shape in shapes], name="finish"
    )(*mlp_0.ends, *mlp_1.ends)
    d_qkv = d_qkv.transpose(0, 2, 1, 3)
    d_proj = d_proj.transpose(0, 2, 1)
    d_fc2 = d_fc2.transpose(0, 2, 1)
    return (
        block_output,
        grad,
        d_qkv,
        d_bqv,
        d_table,
        d_proj,
        d_fc1,
        d_b1,
        d_fc2,
        d_norm,
    )


def solution(mesh):
    in_specs = (
        P(("dp", "tensor"), None),
        P(("dp", "tensor"), None),
        P(None, "dp", None, "tensor"),
        P(None, None, "tensor"),
        P(None, None, "tensor"),
        P(None, "tensor", "dp"),
        P(None, "dp", "tensor"),
        P(None, "tensor"),
        P(None, "tensor", "dp"),
        P(None, None, "dp"),
        P(),
        P(),
        P(),
    )
    out_specs = (
        P(("dp", "tensor"), None),
        P(("dp", "tensor"), None),
        P(None, "dp", None, "tensor"),
        P(None, None, "tensor"),
        P(None, None, "tensor"),
        P(None, "tensor", "dp"),
        P(None, "dp", "tensor"),
        P(None, "tensor"),
        P(None, "tensor", "dp"),
        P(None, None, "dp"),
    )
    return jax.shard_map(body, mesh=mesh, in_specs=in_specs, out_specs=out_specs, check_vma=False)
```
